512 devices in a mesh: section: 32 (over z, core), tensor: 16 (over x, y).
Axes of the slice: x: 4, y: 4, z: 16, core: 2. Of those that a mesh axis runs over, the one named last changes fastest.
Arguments:
- activations: bfloat16 [32, 512, 4096], P('section', None, 'tensor'), may hold values from -48 to 48
- gain: bfloat16 [32, 4096], P('section', 'tensor'), may hold values from 0.5 to 1.5
- w_query: bfloat16 [32, 4096, 4096], P('section', None, 'tensor'), may hold values from -0.0625 to 0.0625
- w_kv: bfloat16 [32, 1024, 4096], P('section', 'tensor'), may hold values from -1.8782524 to 1.8782524
- segments: int32 [32, 512], replicated, may hold values from 0 to 31, never falling along the last dimension, each value on 1 to 128 neighbouring positions
- pool: bfloat16 [64, 128, 4096], P('section', None, 'tensor'), may hold values from -48 to 48
- row_ids: int32 [32], replicated, may hold values from 0 to 63, as said below
- row_lengths: int32 [32], replicated, may hold values from 1 to 128, 512 in all
Outputs:
- after_first: bfloat16 [32, 512, 4096], P('section', None, 'tensor')
- after_second: bfloat16 [32, 512, 4096], P('section', None, 'tensor')
The draws below stay inside these ranges and needn't reach their ends.
Inputs may be any that keep to these rules, and one draw needn't show every extreme that they name: `row_ids`: every block of 2 consecutive ids, the rows of one buffer host, is named at least once; ids may repeat.
All inputs are finite; a program needn't handle non-finite values.
Results may differ from the reference program's by a relative error of at most 0.01.
Values may be sent and summed in bfloat16 or wider, within the bound.
No kernel may reach another device: no remote copies, remote signals or barrier semaphores. Data moves between devices by JAX's collectives and lax.ppermute only.
A program may use at most 64 MiB of HBM per device.

```python
import math
import jax
import jax.numpy as jnp
import numpy as np
from jax import lax

D = 4096
HEADS = 32
KV_HEADS = 4
HEAD_DIM = 128
TOKENS_MB = 512
ROWS_MB = 32
ROW_MAX = 128
HOST_ROWS = 2
LAYERS = 32
POOL_ROWS = 64


def rough_field(key, lead_dim, row_count, col_count):
    sub_keys = jax.random.split(key, 4)
    col_place = jnp.arange(col_count, dtype=jnp.float32) / col_count
    base_vals = jnp.clip(jax.random.normal(sub_keys[0], (lead_dim, row_count, col_count), jnp.float32), -4.0, 4.0)
    col_trend = jnp.exp(math.log(3.0) * (col_place - 0.5))
    row_scale = jnp.exp(jax.random.uniform(sub_keys[2], (lead_dim, row_count, 1), jnp.float32, math.log(0.3), math.log(3.0)))
    col_scale = jnp.exp(jax.random.uniform(sub_keys[3], (lead_dim, 1, col_count), jnp.float32, -0.5 * math.log(10.0), 0.5 * math.log(10.0)))
    values_out = base_vals * row_scale * col_scale * col_trend[None, None, :]
    return jnp.clip(values_out, -48.0, 48.0)


def query_head(key, head_number):
    raw_vals = jax.random.normal(jax.random.fold_in(key, 100 + head_number), (LAYERS, D, HEAD_DIM), jnp.float32)
    return jnp.clip(raw_vals, -4.0, 4.0) * D ** (-0.5)


def draw_activations(key, part):
    return rough_field(jax.random.fold_in(key, 1), LAYERS, TOKENS_MB, D).astype(jnp.bfloat16)


def draw_pool(key, part):
    return rough_field(jax.random.fold_in(key, 2), POOL_ROWS, ROW_MAX, D).astype(jnp.bfloat16)


def draw_w_query(key, part):
    blocks = [query_head(key, head_number) for head_number in range(HEADS)]
    return jnp.concatenate(blocks, axis=2).astype(jnp.bfloat16)


def draw_w_kv(key, part):
    raw_vals = jax.random.normal(jax.random.fold_in(key, 5), (LAYERS, 2 * KV_HEADS * HEAD_DIM, D), jnp.float32)
    weights_out = jnp.clip(raw_vals, -4.0, 4.0) * D ** (-0.5)
    return weights_out.astype(jnp.bfloat16)


def draw_row_ids(key, part):
    sub_keys = jax.random.split(jax.random.fold_in(key, 9), 4)
    host_count = POOL_ROWS // HOST_ROWS
    extra_count = ROWS_MB - host_count
    hosts_first = jax.random.permutation(sub_keys[0], host_count).astype(jnp.int32)
    hosts_extra = jax.random.randint(sub_keys[1], (extra_count,), 0, host_count).astype(jnp.int32)
    local_first = jnp.where(hosts_first == 0, 0, HOST_ROWS - 1).astype(jnp.int32)
    local_extra = jax.random.randint(sub_keys[2], (extra_count,), 0, HOST_ROWS).astype(jnp.int32)
    shuffle_order = jax.random.permutation(sub_keys[3], ROWS_MB)
    host_all = jnp.concatenate([hosts_first, hosts_extra])[shuffle_order]
    local_all = jnp.concatenate([local_first, local_extra])[shuffle_order]
    return (host_all * HOST_ROWS + local_all).astype(jnp.int32)


def split_up(amount, total, most, lean):
    loads = [(1 << 20) // math.isqrt(rank ** lean) + 1 for rank in range(2, amount + 1)]
    rest, holding = total - most - (amount - 1), [1] * (amount - 1)
    while rest > 0:
        candidates = [i for i in range(amount - 1) if holding[i] < most]
        whole, budget = sum([loads[i] for i in candidates]), rest
        for i in candidates:
            addition = min(most - holding[i], max(1, budget * loads[i] // whole), rest)
            holding[i] = holding[i] + addition
            rest = rest - addition
    return np.array([most] + holding)


def ragged_sizes(key, number_of, total, limit, lean):
    if number_of == 2:
        one = jax.random.randint(key, (), max(1, total - limit), min(limit, total - 1) + 1)
        return jnp.stack([one, total - one])
    tallies = jnp.asarray(split_up(number_of, total, limit, lean), jnp.int32)
    couples = (number_of - 1) // 2
    source_of, receiver = tallies[1:1 + 2 * couples:2], tallies[2:2 + 2 * couples:2]
    slack = jnp.minimum(source_of - 1, limit - receiver)
    moved = jax.random.randint(jax.random.fold_in(key, 1), (couples,), 0, 1 << 20) % (slack + 1)
    tallies = tallies.at[1:1 + 2 * couples:2].set(source_of - moved).at[2:2 + 2 * couples:2].set(receiver + moved)
    return tallies[jax.random.permutation(jax.random.fold_in(key, 2), number_of)]


def setup_inputs(seed: int = 0) -> dict:
    arg_keys = jax.random.split(jax.random.key(seed), 9)
    activations = draw_activations(jax.random.fold_in(arg_keys[8], 71), 0)
    gain = jnp.clip(1.0 + 0.1 * jax.random.normal(arg_keys[1], (LAYERS, D), jnp.float32), 0.5, 1.5).astype(jnp.bfloat16)
    w_query = draw_w_query(jax.random.fold_in(arg_keys[8], 71), 0)
    w_kv = draw_w_kv(jax.random.fold_in(arg_keys[8], 71), 0)
    segments = jax.vmap(lambda own: jnp.searchsorted(jnp.cumsum(ragged_sizes(own, ROWS_MB, TOKENS_MB, ROW_MAX, 2)), jnp.arange(TOKENS_MB), side="right"))(jax.random.split(arg_keys[4], LAYERS)).reshape((LAYERS, TOKENS_MB)).astype(jnp.int32)
    pool = draw_pool(jax.random.fold_in(arg_keys[8], 71), 0)
    row_ids = draw_row_ids(jax.random.fold_in(arg_keys[8], 71), 0)
    row_lengths = ragged_sizes(arg_keys[7], ROWS_MB, TOKENS_MB, ROW_MAX, 2).astype(jnp.int32)
    return dict(activations=activations, gain=gain, w_query=w_query, w_kv=w_kv, segments=segments, pool=pool, row_ids=row_ids, row_lengths=row_lengths)


norm_eps = 1e-05
masked_score = -1e+30

def attend_layer(inputs, gain_row, query_weight, keyval_weight, seg_ids):
    row_count = inputs.shape[0]
    wide_inputs = inputs.astype(jnp.float32)
    mean_square = lax.optimization_barrier(jnp.mean(wide_inputs * wide_inputs, axis=1, keepdims=True))
    normed = (wide_inputs * lax.rsqrt(mean_square + norm_eps) * gain_row.astype(jnp.float32)[None, :]).astype(jnp.bfloat16)
    query = jnp.dot(normed, query_weight, preferred_element_type=jnp.float32).astype(jnp.bfloat16)
    keyval = jnp.dot(normed, keyval_weight.T, preferred_element_type=jnp.float32).astype(jnp.bfloat16)
    query = query.reshape(row_count, HEADS, HEAD_DIM).astype(jnp.float32)
    keyval = keyval.reshape(row_count, KV_HEADS, 2, HEAD_DIM).astype(jnp.float32)
    group_size = HEADS // KV_HEADS
    key_heads = jnp.repeat(keyval[:, :, 0], group_size, axis=1)
    value_heads = jnp.repeat(keyval[:, :, 1], group_size, axis=1)
    positions = jnp.arange(row_count, dtype=jnp.int32)
    allowed = (seg_ids[:, None] == seg_ids[None, :]) & (positions[None, :] <= positions[:, None])
    scores = jnp.einsum('rhd,shd->hrs', query, key_heads, precision=lax.Precision.HIGHEST) * HEAD_DIM ** (-0.5)
    scores = jnp.where(allowed[None, :, :], scores, masked_score)
    weights = jax.nn.softmax(scores, axis=-1).astype(jnp.bfloat16)
    context = jnp.einsum('hrs,shd->rhd', weights.astype(jnp.float32), value_heads, precision=lax.Precision.HIGHEST)
    context = context.astype(jnp.bfloat16).reshape(row_count, HEADS * HEAD_DIM)
    return (wide_inputs + context.astype(jnp.float32)).astype(jnp.bfloat16)

def run_sections(packed):
    return attend_layer(packed[0], packed[1], packed[2], packed[3], packed[4])

def reference(activations, gain, w_query, w_kv, segments, pool, row_ids, row_lengths):
    after_first = lax.map(run_sections, (activations, gain, w_query, w_kv, segments))
    token_count = activations.shape[1]
    ends = jnp.cumsum(row_lengths).astype(jnp.int32)
    positions = jnp.arange(token_count, dtype=jnp.int32)
    slot = lax.optimization_barrier(jnp.sum((positions[:, None] >= ends[None, :]).astype(jnp.int32), axis=1)).astype(jnp.int32)
    offset = (positions - ends[slot] + row_lengths[slot]).astype(jnp.int32)
    source = (row_ids[slot] * pool.shape[1] + offset).astype(jnp.int32)
    fresh = pool.reshape(-1, pool.shape[2])[source]
    second_inputs = jnp.concatenate([fresh[None], after_first[:-1]], axis=0)
    second_segments = jnp.concatenate([slot[None], segments[:-1]], axis=0).astype(jnp.int32)
    after_second = lax.map(run_sections, (second_inputs, gain, w_query, w_kv, second_segments))
    return (after_first, after_second)
```

```python
import functools

import jax
import jax.numpy as jnp
from jax import lax
from jax.experimental import pallas as pl
from jax.experimental.pallas import tpu as pltpu
from jax.sharding import PartitionSpec as P

D = 4096
HEAD_DIM = 128
SIDE = 4
BLOCK = 256
KV_ROWS = 64
TOKENS = 512
HALF = 256
ROW_MAX = 128
HOST_ROWS = 2
SLOTS = 32
SENT_ROWS = TOKENS + 2 * KV_ROWS + 16
AXES = ("section", "tensor")
norm_eps = 1e-05
masked_score = -1e30
f32, bf16 = jnp.float32, jnp.bfloat16
VMEM = pl.BlockSpec(memory_space=pltpu.VMEM)
SMEM = pl.BlockSpec(memory_space=pltpu.SMEM)
NT = (((1,), (1,)), ((), ()))


def place(section, first, second):
    return SIDE * first + second if section % 2 == 0 else SIDE * second + first


def rings(sections, along_a):
    groups = []
    for s in range(sections):
        for i in range(SIDE):
            ring = [(place(s, j, i) if along_a else place(s, i, j)) for j in range(SIDE)]
            groups.append([s * SIDE * SIDE + t for t in ring])
    return groups


def head_rings(sections):
    return [[(s * SIDE + g) * SIDE + i for i in range(SIDE)] for s in range(sections) for g in range(SIDE)]


def call(body, out_shape, operands, specs, flops, moved, **more):
    return pl.pallas_call(
        body,
        out_shape=out_shape,
        in_specs=specs,
        out_specs=jax.tree.map(lambda _: VMEM, out_shape),
        compiler_params=pltpu.CompilerParams(vmem_limit_bytes=48 << 20),
        cost_estimate=pl.CostEstimate(flops=flops, bytes_accessed=moved, transcendentals=0),
        **more,
    )(*operands)


def pack_body(odd_ref, query_ref, keyval_ref, out_ref):
    out_ref[0, 0, :BLOCK] = query_ref[...]
    out_ref[0, 0, BLOCK:] = keyval_ref[...]


def pack_weights(odd, w_query, w_kv):
    def source(i, j, odd_ref):
        return jnp.where(odd_ref[0] == 1, SIDE * i + j, SIDE * j + i)

    return pl.pallas_call(
        pack_body,
        out_shape=jax.ShapeDtypeStruct((SIDE, SIDE, BLOCK + KV_ROWS, BLOCK), bf16),
        grid_spec=pltpu.PrefetchScalarGridSpec(
            num_scalar_prefetch=1,
            grid=(SIDE, SIDE),
            in_specs=[
                pl.BlockSpec((BLOCK, BLOCK), lambda i, j, o: (source(i, j, o), 0)),
                pl.BlockSpec((KV_ROWS, BLOCK), lambda i, j, o: (0, source(i, j, o))),
            ],
            out_specs=pl.BlockSpec((1, 1, BLOCK + KV_ROWS, BLOCK), lambda i, j, o: (i, j, 0, 0)),
        ),
        cost_estimate=pl.CostEstimate(flops=0, bytes_accessed=5 << 20, transcendentals=0),
    )(odd, w_query, w_kv)


def project_body(x_ref, gain_ref, w_ref, out_ref, wide_ref, kv_ref):
    ones = jnp.ones((8, BLOCK), bf16)
    squares = jnp.zeros((8, TOKENS), f32)
    for a in range(SIDE):
        part = x_ref[a, :TOKENS].astype(f32)
        gain = gain_ref[a, TOKENS : TOKENS + 1].astype(f32)
        wide_ref[:, a * BLOCK : (a + 1) * BLOCK] = (part * gain).astype(bf16)
        square = part * part
        upper = square.astype(bf16)
        lower = (square - upper.astype(f32)).astype(bf16)
        squares += lax.dot_general(ones, upper, NT, preferred_element_type=f32)
        squares += lax.dot_general(ones, lower, NT, preferred_element_type=f32)
        for b in range(SIDE):
            kv_ref[b * KV_ROWS : (b + 1) * KV_ROWS, a * BLOCK : (a + 1) * BLOCK] = w_ref[b, a, BLOCK:]
    keyval = lax.dot_general(kv_ref[...], wide_ref[...], NT, preferred_element_type=f32).astype(bf16)
    first = squares.astype(bf16)
    second = (squares - first.astype(f32)).astype(bf16)
    stats = [first[:1, :HALF], first[:1, HALF:], second[:1, :HALF], second[:1, HALF:]]
    stats = jnp.concatenate([s.astype(f32) for s in stats] + [jnp.zeros((12, HALF), f32)], axis=0).astype(bf16)
    for b in range(SIDE):
        total = jnp.zeros((TOKENS, BLOCK), f32)
        for a in range(SIDE):
            total += jnp.dot(
                wide_ref[:, a * BLOCK : (a + 1) * BLOCK], w_ref[b, a, :BLOCK], preferred_element_type=f32
            )
        out_ref[b, :TOKENS] = total.astype(bf16)
        rows = slice(b * KV_ROWS, (b + 1) * KV_ROWS)
        out_ref[b, TOKENS : TOKENS + KV_ROWS] = keyval[rows, :HALF]
        out_ref[b, TOKENS + KV_ROWS : TOKENS + 2 * KV_ROWS] = keyval[rows, HALF:]
        out_ref[b, TOKENS + 2 * KV_ROWS :] = stats


def project(x, gain_rows, weights):
    return call(
        project_body,
        jax.ShapeDtypeStruct((SIDE, SENT_ROWS, BLOCK), bf16),
        (x, gain_rows, weights),
        [VMEM] * 3,
        2 * TOKENS * 1024 * 1280,
        6 << 20,
        scratch_shapes=[pltpu.VMEM((TOKENS, SIDE * BLOCK), bf16), pltpu.VMEM((SIDE * KV_ROWS, SIDE * BLOCK), bf16)],
    )


def down(row):
    return jnp.transpose(jnp.broadcast_to(row, (HEAD_DIM, HEAD_DIM)))


def combine_body(parts_ref, query_ref, keyval_ref):
    tail = parts_ref[0, TOKENS:].astype(f32)
    for b in range(1, SIDE):
        tail += parts_ref[b, TOKENS:].astype(f32)
    stats = tail[2 * KV_ROWS :]
    for h in range(2):
        mean = (stats[h : h + 1] + stats[2 + h : 3 + h]) / D
        scale = lax.rsqrt(mean + norm_eps)
        keyval_ref[:, h * HALF : (h + 1) * HALF] = (tail[h * KV_ROWS : (h + 1) * KV_ROWS] * scale).astype(bf16)
        for q in range(2):
            start = h * HALF + q * HEAD_DIM
            rows = slice(start, start + HEAD_DIM)
            total = parts_ref[0, rows].astype(f32)
            for b in range(1, SIDE):
                total += parts_ref[b, rows].astype(f32)
            factor = down(scale[:, q * HEAD_DIM : (q + 1) * HEAD_DIM])
            query_ref[rows] = (total * jnp.concatenate([factor, factor], axis=1)).astype(bf16)


def combine(parts):
    return call(
        combine_body,
        (jax.ShapeDtypeStruct((TOKENS, BLOCK), bf16), jax.ShapeDtypeStruct((KV_ROWS, TOKENS), bf16)),
        (parts,),
        [VMEM],
        TOKENS * BLOCK * 8,
        2 << 20,
    )


def attend_body(is_second, number_ref, lengths_ref, x_ref, query_ref, keyval_ref, segments_ref, out_ref):
    section = number_ref[0]
    if is_second:
        ids = segments_ref[pl.ds(jnp.maximum(section - 1, 0), 1), :]
        spot = lax.broadcasted_iota(jnp.int32, (1, TOKENS), 1)

        def count(k, carried):
            end, slot = carried
            end = end + lengths_ref[k]
            return end, slot + (spot >= end).astype(jnp.int32)

        _, slot = lax.fori_loop(0, SLOTS, count, (jnp.int32(0), jnp.zeros((1, TOKENS), jnp.int32)))
        ids = jnp.where(section == 0, slot, ids)
    else:
        ids = segments_ref[pl.ds(section, 1), :]
    ids = ids.astype(f32)
    for i in range(TOKENS // HEAD_DIM):
        rows = slice(i * HEAD_DIM, (i + 1) * HEAD_DIM)
        low = max(i - 1, 0) * HEAD_DIM
        width = (i + 1) * HEAD_DIM - low
        cols = slice(low, low + width)
        own = down(ids[:, rows])
        if width > HEAD_DIM:
            own = jnp.concatenate([own, own], axis=1)
        place_r = lax.broadcasted_iota(jnp.int32, (HEAD_DIM, width), 0) + i * HEAD_DIM
        place_c = lax.broadcasted_iota(jnp.int32, (HEAD_DIM, width), 1) + low
        allowed = (own == ids[:, cols]) & (place_c <= place_r)
        keys = keyval_ref[:HEAD_DIM, cols]
        values = keyval_ref[HEAD_DIM:, cols]
        for h in range(2):
            lanes = slice(h * HEAD_DIM, (h + 1) * HEAD_DIM)
            scores = jnp.dot(query_ref[rows, lanes], keys, preferred_element_type=f32) * HEAD_DIM ** (-0.5)
            scores = jnp.where(allowed, scores, masked_score)
            grown = jnp.exp(scores - jnp.max(scores, axis=1, keepdims=True))
            weights = (grown / jnp.sum(grown, axis=1, keepdims=True)).astype(bf16)
            context = lax.dot_general(weights, values, NT, preferred_element_type=f32).astype(bf16)
            out_ref[rows, lanes] = (x_ref[rows, lanes].astype(f32) + context.astype(f32)).astype(bf16)


def attend(is_second, number, lengths, x, query, keyval, segments):
    return call(
        functools.partial(attend_body, is_second),
        jax.ShapeDtypeStruct((TOKENS, BLOCK), bf16),
        (number, lengths, x, query, keyval, segments),
        [SMEM, SMEM] + [VMEM] * 4,
        2 * TOKENS * 256 * 128 * 4,
        1 << 20,
    )


def frame_body(number_ref, ids_ref, lengths_ref, pool_ref, out_ref, total_ref):
    total_ref[...] = jnp.zeros_like(total_ref)
    section = number_ref[0]
    row = lax.broadcasted_iota(jnp.int32, (TOKENS, ROW_MAX), 0)
    col = lax.broadcasted_iota(jnp.int32, (TOKENS, ROW_MAX), 1)

    def take(k, start):
        length = lengths_ref[k]
        which = ids_ref[k] - HOST_ROWS * section

        @pl.when((which >= 0) & (which < HOST_ROWS))
        def _():
            hit = ((row - start == col) & (col < length)).astype(f32).astype(bf16)
            total_ref[...] += jnp.dot(hit, pool_ref[which], preferred_element_type=f32)

        return start + length

    lax.fori_loop(0, SLOTS, take, jnp.int32(0))
    out_ref[...] = total_ref[...].astype(bf16)


def make_frame(number, row_ids, row_lengths, pool):
    return call(
        frame_body,
        jax.ShapeDtypeStruct((TOKENS, BLOCK), bf16),
        (number, row_ids, row_lengths, pool),
        [SMEM, SMEM, SMEM, VMEM],
        2 * TOKENS * 128 * 256,
        1 << 20,
        scratch_shapes=[pltpu.VMEM((TOKENS, BLOCK), f32)],
    )


def tree_step(frame, sections, level):
    step = 1 << level
    last = sections - 1
    route = [(i, i + step) for i in range(sections) if (last - i) % (2 * step) == step]
    return frame + lax.ppermute(frame, "section", route)


def per_device(activations, gain, w_query, w_kv, segments, pool, row_ids, row_lengths):
    sections = lax.axis_size("section")
    section = lax.axis_index("section").astype(jnp.int32)
    number = section[None]
    ring_a, ring_b, ring_y = rings(sections, True), rings(sections, False), head_rings(sections)

    def exchange(array, groups):
        return lax.all_to_all(array, AXES, 0, 0, axis_index_groups=groups)

    x = activations[0]
    packed = pack_weights(number % 2, w_query[0], w_kv[0])
    weights = exchange(packed, ring_b)
    own = jnp.concatenate([x, jnp.broadcast_to(gain, (16, BLOCK))], axis=0)
    gathered = exchange(jnp.broadcast_to(own[None], (SIDE,) + own.shape), ring_a)

    frame = make_frame(number, row_ids, row_lengths, pool)
    levels = sections.bit_length() - 1
    for level in range(levels):
        frame = tree_step(frame, sections, level)

    def layer(inputs, blocks, is_second):
        parts = exchange(project(blocks, gathered, weights), ring_b)
        query, keyval = combine(parts)
        keyval = lax.all_gather(keyval, AXES, axis=0, axis_index_groups=ring_y, tiled=True)
        return attend(is_second, number, row_lengths, inputs, query, keyval, segments)

    first = layer(x, gathered, False)
    sent = jnp.where(section == sections - 1, frame, first)
    route = [(i, (i + 1) % sections) for i in range(sections)]
    handed = lax.ppermute(sent, "section", route)
    blocks = exchange(jnp.broadcast_to(handed[None], (SIDE,) + handed.shape), ring_a)
    second = layer(handed, blocks, True)
    return first[None], second[None]


def solution(mesh):
    return jax.shard_map(
        per_device,
        mesh=mesh,
        in_specs=(
            P("section", None, "tensor"),
            P("section", "tensor"),
            P("section", None, "tensor"),
            P("section", "tensor", None),
            P(),
            P("section", None, "tensor"),
            P(),
            P(),
        ),
        out_specs=(P("section", None, "tensor"), P("section", None, "tensor")),
        check_vma=False,
    )
```

```python
import functools

import jax
import jax.numpy as jnp
from jax import lax
from jax.experimental import pallas as pl
from jax.experimental.pallas import tpu as pltpu
from jax.sharding import PartitionSpec as P

D = 4096
HEAD_DIM = 128
SIDE = 4
BLOCK = 256
KV_ROWS = 64
TOKENS = 512
HALF = 256
ROW_MAX = 128
HOST_ROWS = 2
SLOTS = 32
SENT_ROWS = 2 * KV_ROWS + 16
PROJECT_VMEM = 62_500_000
AXES = ("section", "tensor")
norm_eps = 1e-05
masked_score = -1e30
f32, bf16 = jnp.float32, jnp.bfloat16
VMEM = pl.BlockSpec(memory_space=pltpu.VMEM)
ANY = pl.BlockSpec(memory_space=pl.ANY)
SMEM = pl.BlockSpec(memory_space=pltpu.SMEM)
NT = (((1,), (1,)), ((), ()))


def place(section, first, second):
    return SIDE * first + second if section % 2 == 0 else SIDE * second + first


def rings(sections, along_a):
    groups = []
    for s in range(sections):
        for i in range(SIDE):
            ring = [(place(s, j, i) if along_a else place(s, i, j)) for j in range(SIDE)]
            groups.append([s * SIDE * SIDE + t for t in ring])
    return groups


def head_rings(sections):
    return [[(s * SIDE + g) * SIDE + i for i in range(SIDE)] for s in range(sections) for g in range(SIDE)]


def call(body, out_shape, operands, specs, flops, moved, out_specs=None, vmem=12 << 20, **more):
    return pl.pallas_call(
        body,
        out_shape=out_shape,
        in_specs=specs,
        out_specs=out_specs or jax.tree.map(lambda _: VMEM, out_shape),
        compiler_params=pltpu.CompilerParams(vmem_limit_bytes=vmem),
        cost_estimate=pl.CostEstimate(flops=flops, bytes_accessed=moved, transcendentals=0),
        **more,
    )(*operands)


def prepare_body(x_ref, gain_ref, query_ref, keyval_ref, packed_ref, own_ref, gain_rows, sems):
    odd = lax.axis_index("section") % 2
    gain_rows[...] = jnp.broadcast_to(gain_ref[...].astype(f32), (16, BLOCK)).astype(bf16)
    copies = [
        (x_ref, own_ref.at[pl.ds(0, TOKENS)]),
        (gain_rows, own_ref.at[pl.ds(TOKENS, 16)]),
    ]
    for i in range(SIDE):
        for j in range(SIDE):
            start = pl.multiple_of(jnp.where(odd == 1, SIDE * i + j, SIDE * j + i) * BLOCK, BLOCK)
            copies.append((query_ref.at[pl.ds(start, BLOCK)], packed_ref.at[i, j, pl.ds(0, BLOCK)]))
            copies.append((keyval_ref.at[:, pl.ds(start, BLOCK)], packed_ref.at[i, j, pl.ds(BLOCK, KV_ROWS)]))
    copies = [pltpu.make_async_copy(src, dst, sems.at[n]) for n, (src, dst) in enumerate(copies)]
    for copy in copies:
        copy.start()
    for copy in copies:
        copy.wait()


def prepare(x, gain, w_query, w_kv):
    return pl.pallas_call(
        prepare_body,
        out_shape=(
            jax.ShapeDtypeStruct((SIDE, SIDE, BLOCK + KV_ROWS, BLOCK), bf16),
            jax.ShapeDtypeStruct((TOKENS + 16, BLOCK), bf16),
        ),
        in_specs=[ANY, VMEM, ANY, ANY],
        out_specs=(ANY, ANY),
        scratch_shapes=[pltpu.VMEM((16, BLOCK), bf16), pltpu.SemaphoreType.DMA((2 + 2 * SIDE * SIDE,))],
        cost_estimate=pl.CostEstimate(flops=0, bytes_accessed=6 << 20, transcendentals=0),
    )(x, gain, w_query, w_kv)


def ring_place():
    section, tensor = lax.axis_index("section"), lax.axis_index("tensor")
    return jnp.where(section % 2 == 1, tensor % SIDE, tensor // SIDE)


def project_body(is_second, *refs):
    x_refs, gain_refs = refs[:SIDE], refs[SIDE : SIDE + is_second]
    w_hbm, query_ref, keyval_ref, *more, x_ref, w_ref, wide_ref, kv_ref, made_ref, sems = refs[SIDE + len(gain_refs) :]
    x_copies = [pltpu.make_async_copy(x_refs[d], x_ref.at[d], sems.at[d]) for d in range(SIDE)]
    w_copies = [pltpu.make_async_copy(w_hbm.at[b], w_ref.at[b], sems.at[SIDE + b]) for b in range(SIDE)]
    for copy in x_copies + w_copies:
        copy.start()
    here = ring_place()
    origins = [(here + SIDE - d) % SIDE for d in range(SIDE)]
    ones = jnp.ones((8, BLOCK), bf16)
    squares = jnp.zeros((8, TOKENS), f32)
    for d in range(SIDE):
        x_copies[d].wait()
        cols = slice(d * BLOCK, (d + 1) * BLOCK)
        if is_second:
            gain = gain_refs[0][16 * d : 16 * d + 1]
        else:
            gain = x_ref[d, TOKENS : TOKENS + 1]
            more[0][16 * d : 16 * (d + 1)] = x_ref[d, TOKENS:]
        part = x_ref[d, :TOKENS].astype(f32)
        wide_ref[:, cols] = (part * gain.astype(f32)).astype(bf16)
        square = part * part
        upper = square.astype(bf16)
        lower = (square - upper.astype(f32)).astype(bf16)
        squares += lax.dot_general(ones, upper, NT, preferred_element_type=f32)
        squares += lax.dot_general(ones, lower, NT, preferred_element_type=f32)
    copies = []
    for b in range(SIDE):
        w_copies[b].wait()
        for d in range(SIDE):
            kv_ref[b * KV_ROWS : (b + 1) * KV_ROWS, d * BLOCK : (d + 1) * BLOCK] = w_ref[b, origins[d], BLOCK:]
        total = jnp.zeros((TOKENS, BLOCK), f32)
        for d in range(SIDE):
            total += jnp.dot(
                wide_ref[:, d * BLOCK : (d + 1) * BLOCK], w_ref[b, origins[d], :BLOCK], preferred_element_type=f32
            )
        made_ref[b] = total.astype(bf16)
        copy = pltpu.make_async_copy(made_ref.at[b], query_ref.at[b], sems.at[2 * SIDE + b])
        copy.start()
        copies.append(copy)
    keyval = lax.dot_general(kv_ref[...], wide_ref[...], NT, preferred_element_type=f32).astype(bf16)
    first = squares.astype(bf16)
    second = (squares - first.astype(f32)).astype(bf16)
    stats = [first[:1, :HALF], first[:1, HALF:], second[:1, :HALF], second[:1, HALF:]]
    stats = jnp.concatenate([s.astype(f32) for s in stats] + [jnp.zeros((12, HALF), f32)], axis=0).astype(bf16)
    for b in range(SIDE):
        rows = slice(b * KV_ROWS, (b + 1) * KV_ROWS)
        keyval_ref[b, :KV_ROWS] = keyval[rows, :HALF]
        keyval_ref[b, KV_ROWS : 2 * KV_ROWS] = keyval[rows, HALF:]
        keyval_ref[b, 2 * KV_ROWS :] = stats
    for copy in copies:
        copy.wait()


def project(is_second, blocks, gains, weights):
    made = (SIDE, TOKENS, BLOCK)
    out_shape = [jax.ShapeDtypeStruct(made, bf16), jax.ShapeDtypeStruct((SIDE, SENT_ROWS, HALF), bf16)]
    if not is_second:
        out_shape.append(jax.ShapeDtypeStruct((16 * SIDE, BLOCK), bf16))
    return call(
        functools.partial(project_body, is_second),
        tuple(out_shape),
        (*blocks, *gains, weights),
        [ANY] * SIDE + [VMEM] * len(gains) + [ANY],
        2 * TOKENS * 1024 * 1280,
        5 << 20,
        out_specs=(ANY,) + (VMEM,) * (len(out_shape) - 1),
        vmem=PROJECT_VMEM,
        scratch_shapes=[
            pltpu.VMEM((SIDE, *blocks[0].shape), bf16),
            pltpu.VMEM(weights.shape, bf16),
            pltpu.VMEM((TOKENS, SIDE * BLOCK), bf16),
            pltpu.VMEM((SIDE * KV_ROWS, SIDE * BLOCK), bf16),
            pltpu.VMEM(made, bf16),
            pltpu.SemaphoreType.DMA((3 * SIDE,)),
        ],
    )


def down(row):
    return jnp.transpose(jnp.broadcast_to(row, (HEAD_DIM, HEAD_DIM)))


def combine_body(parts_ref, keyval_ref, scale_ref):
    tail = parts_ref[0].astype(f32)
    for b in range(1, SIDE):
        tail += parts_ref[b].astype(f32)
    stats = tail[2 * KV_ROWS :]
    for h in range(2):
        cols = slice(h * HALF, (h + 1) * HALF)
        scale = lax.rsqrt((stats[h : h + 1] + stats[2 + h : 3 + h]) / D + norm_eps)
        keyval_ref[:, cols] = (tail[h * KV_ROWS : (h + 1) * KV_ROWS] * scale).astype(bf16)
        scale_ref[:, cols] = jnp.broadcast_to(scale, (8, HALF))


def combine(parts):
    return call(
        combine_body,
        (jax.ShapeDtypeStruct((KV_ROWS, TOKENS), bf16), jax.ShapeDtypeStruct((8, TOKENS), f32)),
        (parts,),
        [VMEM],
        TOKENS * KV_ROWS * 8,
        1 << 19,
    )


def attend_body(is_second, lengths_ref, x_ref, parts_ref, scale_ref, keyval_ref, segments_ref, *refs):
    section = lax.axis_index("section")
    if is_second:
        (out_ref,) = refs
    else:
        *frame_refs, out_ref, sent_ref, held, sems = refs
    if is_second:
        ids = segments_ref[pl.ds(jnp.maximum(section - 1, 0), 1), :]
        spot = lax.broadcasted_iota(jnp.int32, (1, TOKENS), 1)

        def count(k, carried):
            end, slot = carried
            end = end + lengths_ref[k]
            return end, slot + (spot >= end).astype(jnp.int32)

        _, slot = lax.fori_loop(0, SLOTS, count, (jnp.int32(0), jnp.zeros((1, TOKENS), jnp.int32)))
        ids = jnp.where(section == 0, slot, ids)
    else:
        ids = segments_ref[pl.ds(section, 1), :]
    ids = ids.astype(f32)
    for i in range(TOKENS // HEAD_DIM):
        rows = slice(i * HEAD_DIM, (i + 1) * HEAD_DIM)
        low = max(i - 1, 0) * HEAD_DIM
        width = (i + 1) * HEAD_DIM - low
        cols = slice(low, low + width)
        own = down(ids[:, rows])
        if width > HEAD_DIM:
            own = jnp.concatenate([own, own], axis=1)
        place_r = lax.broadcasted_iota(jnp.int32, (HEAD_DIM, width), 0) + i * HEAD_DIM
        place_c = lax.broadcasted_iota(jnp.int32, (HEAD_DIM, width), 1) + low
        allowed = (own == ids[:, cols]) & (place_c <= place_r)
        total = parts_ref[0, rows].astype(f32)
        for b in range(1, SIDE):
            total += parts_ref[b, rows].astype(f32)
        factor = down(scale_ref[:1, rows])
        query = (total * jnp.concatenate([factor, factor], axis=1)).astype(bf16)
        keys = keyval_ref[:HEAD_DIM, cols]
        values = keyval_ref[HEAD_DIM:, cols]
        for h in range(2):
            lanes = slice(h * HEAD_DIM, (h + 1) * HEAD_DIM)
            scores = jnp.dot(query[:, lanes], keys, preferred_element_type=f32) * HEAD_DIM ** (-0.5)
            scores = jnp.where(allowed, scores, masked_score)
            grown = jnp.exp(scores - jnp.max(scores, axis=1, keepdims=True))
            weights = (grown / jnp.sum(grown, axis=1, keepdims=True)).astype(bf16)
            context = lax.dot_general(weights, values, NT, preferred_element_type=f32).astype(bf16)
            done = (x_ref[rows, lanes].astype(f32) + context.astype(f32)).astype(bf16)
            out_ref[rows, lanes] = done
            if not is_second:
                sent_ref[rows, lanes] = done
    if not is_second:

        @pl.when(section == lax.axis_size("section") - 1)
        def _():
            copies = [pltpu.make_async_copy(ref, held.at[n], sems.at[n]) for n, ref in enumerate(frame_refs)]
            for copy in copies:
                copy.start()
            for copy in copies:
                copy.wait()
            sent_ref[...] = functools.reduce(jnp.add, [held[n].astype(f32) for n in range(SIDE)]).astype(bf16)


def attend(is_second, lengths, x, parts, scale, keyval, segments, frames):
    made = jax.ShapeDtypeStruct((TOKENS, BLOCK), bf16)
    held = pltpu.VMEM((SIDE, TOKENS, BLOCK), bf16)
    scratch = [] if is_second else [held, pltpu.SemaphoreType.DMA((SIDE,))]
    return call(
        functools.partial(attend_body, is_second),
        made if is_second else (made, made),
        (lengths, x, parts, scale, keyval, segments, *frames),
        [SMEM] + [VMEM] * 5 + [ANY] * len(frames),
        2 * TOKENS * 256 * 128 * 4,
        1 << 20,
        scratch_shapes=scratch,
    )


def frame_body(ids_ref, lengths_ref, pool_ref, out_ref, total_ref):
    total_ref[...] = jnp.zeros_like(total_ref)
    section = lax.axis_index("section")
    row = lax.broadcasted_iota(jnp.int32, (TOKENS, ROW_MAX), 0)
    col = lax.broadcasted_iota(jnp.int32, (TOKENS, ROW_MAX), 1)

    def take(k, start):
        length = lengths_ref[k]
        which = ids_ref[k] - HOST_ROWS * section

        @pl.when((which >= 0) & (which < HOST_ROWS))
        def _():
            hit = ((row - start == col) & (col < length)).astype(f32).astype(bf16)
            total_ref[...] += jnp.dot(hit, pool_ref[which], preferred_element_type=f32)

        return start + length

    lax.fori_loop(0, SLOTS, take, jnp.int32(0))
    out_ref[...] = total_ref[...].astype(bf16)


def make_frame(row_ids, row_lengths, pool):
    return call(
        frame_body,
        jax.ShapeDtypeStruct((TOKENS, BLOCK), bf16),
        (row_ids, row_lengths, pool),
        [SMEM, SMEM, VMEM],
        2 * TOKENS * 128 * 256,
        1 << 20,
        scratch_shapes=[pltpu.VMEM((TOKENS, BLOCK), f32)],
    )


def bring(array, sections, step, count=1):
    last, span = sections - 1, (count + 1) * step
    got = []
    for n in range(1, count + 1):
        route = [(i - n * step, i) for i in range(sections) if (last - i) % span == 0]
        got.append(lax.ppermute(array, "section", route))
    return got


def per_device(activations, gain, w_query, w_kv, segments, pool, row_ids, row_lengths):
    sections = lax.axis_size("section")
    ring_b, ring_y = rings(sections, False), head_rings(sections)
    grid = [(s, a, b) for s in range(sections) for a in range(SIDE) for b in range(SIDE)]
    barrier = lax.optimization_barrier

    def number(s, a, b, like):
        return s * SIDE * SIDE + place(like, a % SIDE, b)

    def exchange(array):
        return lax.all_to_all(array, AXES, 0, 0, axis_index_groups=ring_b)

    x = activations[0]
    packed, own = prepare(x, gain, w_query[0], w_kv[0])
    weights = exchange(packed)
    blocks = [own]
    for d in range(1, SIDE):
        route = [(number(s, a - d, b, s), number(s, a, b, s)) for s, a, b in grid]
        blocks.append(lax.ppermute(own, AXES, route))

    blocks, pool = barrier((blocks, pool))
    frame = make_frame(row_ids, row_lengths, pool)
    frame = frame + bring(frame, sections, 1)[0]
    weights, frame = barrier((weights, frame))
    piece = bring(frame, sections, 2)[0]

    query_parts, keyval_parts, gains = project(False, blocks, [], weights)
    query_parts = exchange(query_parts)
    keyval_parts, frame = barrier((keyval_parts, frame + piece))
    piece = bring(frame, sections, 4)[0]
    keyval, scale = combine(exchange(keyval_parts))
    keyval, frame = barrier((keyval, frame + piece))
    frames = [frame, *bring(frame, sections, 8, 3)]
    keyval = lax.all_gather(keyval, AXES, axis=0, axis_index_groups=ring_y, tiled=True)
    first, sent = attend(False, row_lengths, x, query_parts, scale, keyval, segments, frames)

    blocks = []
    for d in range(SIDE):
        route = [(number((s - 1) % sections, a - d, b, s), number(s, a, b, s)) for s, a, b in grid]
        blocks.append(lax.ppermute(sent, AXES, route))
    query_parts, keyval_parts = project(True, blocks, [gains], weights)
    query_parts = exchange(query_parts)
    keyval, scale = combine(exchange(keyval_parts))
    keyval = lax.all_gather(keyval, AXES, axis=0, axis_index_groups=ring_y, tiled=True)
    second = attend(True, row_lengths, blocks[0], query_parts, scale, keyval, segments, [])
    return first[None], second[None]


def solution(mesh):
    return jax.shard_map(
        per_device,
        mesh=mesh,
        in_specs=(
            P("section", None, "tensor"),
            P("section", "tensor"),
            P("section", None, "tensor"),
            P("section", "tensor", None),
            P(),
            P("section", None, "tensor"),
            P(),
            P(),
        ),
        out_specs=(P("section", None, "tensor"), P("section", None, "tensor")),
        check_vma=False,
    )
```

```python
import functools

import jax
import jax.numpy as jnp
from jax import lax
from jax.experimental import pallas as pl
from jax.experimental.pallas import tpu as pltpu
from jax.sharding import PartitionSpec as P

D = 4096
HEAD_DIM = 128
SIDE = 4
BLOCK = 256
KV_ROWS = 64
TOKENS = 512
HALF = 256
ROW_MAX = 128
HOST_ROWS = 2
SLOTS = 32
SENT_ROWS = TOKENS + 2 * KV_ROWS + 16
AXES = ("section", "tensor")
norm_eps = 1e-05
masked_score = -1e30
f32, bf16 = jnp.float32, jnp.bfloat16
VMEM = pl.BlockSpec(memory_space=pltpu.VMEM)
ANY = pl.BlockSpec(memory_space=pl.ANY)
SMEM = pl.BlockSpec(memory_space=pltpu.SMEM)
NT = (((1,), (1,)), ((), ()))


def place(section, first, second):
    return SIDE * first + second if section % 2 == 0 else SIDE * second + first


def rings(sections, along_a):
    groups = []
    for s in range(sections):
        for i in range(SIDE):
            ring = [(place(s, j, i) if along_a else place(s, i, j)) for j in range(SIDE)]
            groups.append([s * SIDE * SIDE + t for t in ring])
    return groups


def head_rings(sections):
    return [[(s * SIDE + g) * SIDE + i for i in range(SIDE)] for s in range(sections) for g in range(SIDE)]


def call(body, out_shape, operands, specs, flops, moved, **more):
    return pl.pallas_call(
        body,
        out_shape=out_shape,
        in_specs=specs,
        out_specs=jax.tree.map(lambda _: VMEM, out_shape),
        compiler_params=pltpu.CompilerParams(vmem_limit_bytes=12 << 20),
        cost_estimate=pl.CostEstimate(flops=flops, bytes_accessed=moved, transcendentals=0),
        **more,
    )(*operands)


def prepare_body(x_ref, gain_ref, query_ref, keyval_ref, packed_ref, own_ref, packed, own, sems):
    odd = lax.axis_index("section") % 2
    arrivals = []
    for i in range(SIDE):
        for j in range(SIDE):
            start = pl.multiple_of(jnp.where(odd == 1, SIDE * i + j, SIDE * j + i) * BLOCK, BLOCK)
            arrivals.append((query_ref.at[pl.ds(start, BLOCK)], packed.at[i, j, pl.ds(0, BLOCK)]))
            arrivals.append((keyval_ref.at[:, pl.ds(start, BLOCK)], packed.at[i, j, pl.ds(BLOCK, KV_ROWS)]))
    arrivals.append((x_ref, own.at[pl.ds(0, TOKENS)]))
    arrivals = [pltpu.make_async_copy(src, dst, sems.at[n]) for n, (src, dst) in enumerate(arrivals)]
    for copy in arrivals:
        copy.start()
    own[TOKENS:] = jnp.broadcast_to(gain_ref[...].astype(f32), (16, BLOCK)).astype(bf16)
    leaving = []
    for i in range(SIDE + 1):
        for copy in arrivals[2 * SIDE * i : 2 * SIDE * (i + 1)]:
            copy.wait()
        src, dst = (packed.at[i], packed_ref.at[i]) if i < SIDE else (own, own_ref)
        leaving.append(pltpu.make_async_copy(src, dst, sems.at[len(arrivals) + i]))
        leaving[-1].start()
    for copy in leaving:
        copy.wait()


def prepare(x, gain, w_query, w_kv):
    packed = (SIDE, SIDE, BLOCK + KV_ROWS, BLOCK)
    own = (TOKENS + 16, BLOCK)
    return pl.pallas_call(
        prepare_body,
        out_shape=(jax.ShapeDtypeStruct(packed, bf16), jax.ShapeDtypeStruct(own, bf16)),
        in_specs=[ANY, VMEM, ANY, ANY],
        out_specs=(ANY, ANY),
        scratch_shapes=[
            pltpu.VMEM(packed, bf16),
            pltpu.VMEM(own, bf16),
            pltpu.SemaphoreType.DMA((2 * SIDE * SIDE + SIDE + 2,)),
        ],
        cost_estimate=pl.CostEstimate(flops=0, bytes_accessed=6 << 20, transcendentals=0),
    )(x, gain, w_query, w_kv)


def ring_place():
    section, tensor = lax.axis_index("section"), lax.axis_index("tensor")
    return jnp.where(section % 2 == 1, tensor % SIDE, tensor // SIDE)


def project_body(is_second, *refs):
    x_refs = refs[:SIDE]
    if is_second:
        gain_ref, w_ref, out_ref, wide_ref, kv_ref = refs[SIDE:]
    else:
        w_ref, out_ref, gain_ref, wide_ref, kv_ref = refs[SIDE:]
    here = ring_place()
    ones = jnp.ones((8, BLOCK), bf16)
    squares = jnp.zeros((8, TOKENS), f32)
    origins = [(here + SIDE - d) % SIDE for d in range(SIDE)]
    for d in range(SIDE):
        cols = slice(d * BLOCK, (d + 1) * BLOCK)
        if not is_second:
            gain_ref[16 * d : 16 * (d + 1)] = x_refs[d][TOKENS:]
        part = x_refs[d][:TOKENS].astype(f32)
        wide_ref[:, cols] = (part * gain_ref[16 * d : 16 * d + 1].astype(f32)).astype(bf16)
        square = part * part
        upper = square.astype(bf16)
        lower = (square - upper.astype(f32)).astype(bf16)
        squares += lax.dot_general(ones, upper, NT, preferred_element_type=f32)
        squares += lax.dot_general(ones, lower, NT, preferred_element_type=f32)
        for b in range(SIDE):
            kv_ref[b * KV_ROWS : (b + 1) * KV_ROWS, cols] = w_ref[b, origins[d], BLOCK:]
    keyval = lax.dot_general(kv_ref[...], wide_ref[...], NT, preferred_element_type=f32).astype(bf16)
    first = squares.astype(bf16)
    second = (squares - first.astype(f32)).astype(bf16)
    stats = [first[:1, :HALF], first[:1, HALF:], second[:1, :HALF], second[:1, HALF:]]
    stats = jnp.concatenate([s.astype(f32) for s in stats] + [jnp.zeros((12, HALF), f32)], axis=0).astype(bf16)
    for b in range(SIDE):
        total = jnp.zeros((TOKENS, BLOCK), f32)
        for d in range(SIDE):
            total += jnp.dot(
                wide_ref[:, d * BLOCK : (d + 1) * BLOCK],
                w_ref[b, origins[d], :BLOCK],
                preferred_element_type=f32,
            )
        out_ref[b, :TOKENS] = total.astype(bf16)
        rows = slice(b * KV_ROWS, (b + 1) * KV_ROWS)
        out_ref[b, TOKENS : TOKENS + KV_ROWS] = keyval[rows, :HALF]
        out_ref[b, TOKENS + KV_ROWS : TOKENS + 2 * KV_ROWS] = keyval[rows, HALF:]
        out_ref[b, TOKENS + 2 * KV_ROWS :] = stats


def project(is_second, blocks, gains, weights):
    parts = jax.ShapeDtypeStruct((SIDE, SENT_ROWS, BLOCK), bf16)
    return call(
        functools.partial(project_body, is_second),
        parts if is_second else (parts, jax.ShapeDtypeStruct((16 * SIDE, BLOCK), bf16)),
        (*blocks, *gains, weights),
        [VMEM] * (SIDE + len(gains) + 1),
        2 * TOKENS * 1024 * 1280,
        6 << 20,
        scratch_shapes=[pltpu.VMEM((TOKENS, SIDE * BLOCK), bf16), pltpu.VMEM((SIDE * KV_ROWS, SIDE * BLOCK), bf16)],
    )


def down(row):
    return jnp.transpose(jnp.broadcast_to(row, (HEAD_DIM, HEAD_DIM)))


def combine_body(parts_ref, query_ref, keyval_ref):
    tail = parts_ref[0, TOKENS:].astype(f32)
    for b in range(1, SIDE):
        tail += parts_ref[b, TOKENS:].astype(f32)
    stats = tail[2 * KV_ROWS :]
    for h in range(2):
        mean = (stats[h : h + 1] + stats[2 + h : 3 + h]) / D
        scale = lax.rsqrt(mean + norm_eps)
        keyval = (tail[h * KV_ROWS : (h + 1) * KV_ROWS] * scale).astype(bf16)
        for b in range(SIDE):
            keyval_ref[b, :, h * HALF : (h + 1) * HALF] = keyval
        for q in range(2):
            start = h * HALF + q * HEAD_DIM
            rows = slice(start, start + HEAD_DIM)
            total = parts_ref[0, rows].astype(f32)
            for b in range(1, SIDE):
                total += parts_ref[b, rows].astype(f32)
            factor = down(scale[:, q * HEAD_DIM : (q + 1) * HEAD_DIM])
            query_ref[rows] = (total * jnp.concatenate([factor, factor], axis=1)).astype(bf16)


def combine(parts):
    return call(
        combine_body,
        (jax.ShapeDtypeStruct((TOKENS, BLOCK), bf16), jax.ShapeDtypeStruct((SIDE, KV_ROWS, TOKENS), bf16)),
        (parts,),
        [VMEM],
        TOKENS * BLOCK * 8,
        2 << 20,
    )


def attend_body(is_second, lengths_ref, x_ref, query_ref, keyval_ref, segments_ref, *refs):
    section = lax.axis_index("section")
    if is_second:
        (out_ref,) = refs
    else:
        *frame_refs, out_ref, sent_ref, held, sems = refs
    if is_second:
        ids = segments_ref[pl.ds(jnp.maximum(section - 1, 0), 1), :]
        spot = lax.broadcasted_iota(jnp.int32, (1, TOKENS), 1)

        def count(k, carried):
            end, slot = carried
            end = end + lengths_ref[k]
            return end, slot + (spot >= end).astype(jnp.int32)

        _, slot = lax.fori_loop(0, SLOTS, count, (jnp.int32(0), jnp.zeros((1, TOKENS), jnp.int32)))
        ids = jnp.where(section == 0, slot, ids)
    else:
        ids = segments_ref[pl.ds(section, 1), :]
    ids = ids.astype(f32)
    steps = []
    for i in range(TOKENS // HEAD_DIM):
        rows = slice(i * HEAD_DIM, (i + 1) * HEAD_DIM)
        low = max(i - 1, 0) * HEAD_DIM
        width = (i + 1) * HEAD_DIM - low
        cols = slice(low, low + width)
        own = down(ids[:, rows])
        if width > HEAD_DIM:
            own = jnp.concatenate([own, own], axis=1)
        place_r = lax.broadcasted_iota(jnp.int32, (HEAD_DIM, width), 0) + i * HEAD_DIM
        place_c = lax.broadcasted_iota(jnp.int32, (HEAD_DIM, width), 1) + low
        allowed = (own == ids[:, cols]) & (place_c <= place_r)
        keys = jnp.concatenate([keyval_ref[0, :, cols], keyval_ref[1, :, cols]], axis=0)
        for h in range(2):
            lanes = slice(h * HEAD_DIM, (h + 1) * HEAD_DIM)
            scores = jnp.dot(query_ref[rows, lanes], keys, preferred_element_type=f32) * HEAD_DIM ** (-0.5)
            steps.append((rows, cols, lanes, jnp.where(allowed, scores, masked_score)))
    for n, (rows, cols, lanes, scores) in enumerate(steps):
        grown = jnp.exp(scores - jnp.max(scores, axis=1, keepdims=True))
        weights = (grown * (1.0 / jnp.sum(grown, axis=1, keepdims=True))).astype(bf16)
        steps[n] = (rows, cols, lanes, weights)
    for rows, cols, lanes, weights in steps:
        values = jnp.concatenate([keyval_ref[2, :, cols], keyval_ref[3, :, cols]], axis=0)
        context = lax.dot_general(weights, values, NT, preferred_element_type=f32).astype(bf16)
        done = (x_ref[rows, lanes].astype(f32) + context.astype(f32)).astype(bf16)
        out_ref[rows, lanes] = done
        if not is_second:
            sent_ref[rows, lanes] = done
    if not is_second:

        @pl.when(section == lax.axis_size("section") - 1)
        def _():
            copies = [pltpu.make_async_copy(ref, held.at[n], sems.at[n]) for n, ref in enumerate(frame_refs)]
            for copy in copies:
                copy.start()
            for copy in copies:
                copy.wait()
            sent_ref[...] = functools.reduce(jnp.add, [held[n].astype(f32) for n in range(SIDE)]).astype(bf16)


def attend(is_second, lengths, x, query, keyval, segments, frames):
    made = jax.ShapeDtypeStruct((TOKENS, BLOCK), bf16)
    held = pltpu.VMEM((SIDE, TOKENS, BLOCK), bf16)
    return call(
        functools.partial(attend_body, is_second),
        made if is_second else (made, made),
        (lengths, x, query, keyval, segments, *frames),
        [SMEM] + [VMEM] * 4 + [ANY] * len(frames),
        2 * TOKENS * 256 * 128 * 4,
        1 << 20,
        scratch_shapes=[] if is_second else [held, pltpu.SemaphoreType.DMA((SIDE,))],
    )


def frame_body(ids_ref, lengths_ref, pool_ref, out_ref, total_ref):
    total_ref[...] = jnp.zeros_like(total_ref)
    section = lax.axis_index("section")
    row = lax.broadcasted_iota(jnp.int32, (TOKENS, ROW_MAX), 0)
    col = lax.broadcasted_iota(jnp.int32, (TOKENS, ROW_MAX), 1)

    def take(k, start):
        length = lengths_ref[k]
        which = ids_ref[k] - HOST_ROWS * section

        @pl.when((which >= 0) & (which < HOST_ROWS))
        def _():
            hit = ((row - start == col) & (col < length)).astype(f32).astype(bf16)
            total_ref[...] += jnp.dot(hit, pool_ref[which], preferred_element_type=f32)

        return start + length

    lax.fori_loop(0, SLOTS, take, jnp.int32(0))
    out_ref[...] = total_ref[...].astype(bf16)


def make_frame(row_ids, row_lengths, pool):
    return call(
        frame_body,
        jax.ShapeDtypeStruct((TOKENS, BLOCK), bf16),
        (row_ids, row_lengths, pool),
        [SMEM, SMEM, VMEM],
        2 * TOKENS * 128 * 256,
        1 << 20,
        scratch_shapes=[pltpu.VMEM((TOKENS, BLOCK), f32)],
    )


def bring(array, sections, step, count):
    last = sections - 1
    got = []
    for n in range(1, count + 1):
        route = [(i - n * step, i) for i in range(sections) if (last - i) % ((count + 1) * step) == 0]
        got.append(lax.ppermute(array, "section", route))
    return got


def total_of(arrays):
    total = arrays[0].astype(f32)
    for array in arrays[1:]:
        total = total + array.astype(f32)
    return total.astype(bf16)


def per_device(activations, gain, w_query, w_kv, segments, pool, row_ids, row_lengths):
    sections = lax.axis_size("section")
    ring_b, ring_y = rings(sections, False), head_rings(sections)
    barrier = lax.optimization_barrier
    grid = [(s, a, b) for s in range(sections) for a in range(SIDE) for b in range(SIDE)]

    def number(s, a, b, like):
        return s * SIDE * SIDE + place(like, a % SIDE, b)

    def exchange(array, ring):
        return lax.all_to_all(array, AXES, 0, 0, axis_index_groups=ring)

    x = activations[0]
    packed, own = prepare(x, gain, w_query[0], w_kv[0])
    weights = exchange(packed, ring_b)
    blocks = [own]
    for d in range(1, SIDE):
        route = [(number(s, a - d, b, s), number(s, a, b, s)) for s, a, b in grid]
        blocks.append(lax.ppermute(own, AXES, route))

    blocks, pool = barrier((blocks, pool))
    frame = make_frame(row_ids, row_lengths, pool)
    frame = frame + bring(frame, sections, 1, 1)[0]
    weights, frame = barrier((weights, frame))
    pieces = bring(frame, sections, 2, 3)

    parts, gains = project(False, blocks, [], weights)
    parts = exchange(parts, ring_b)
    frame = total_of([frame, *pieces])
    parts, frame = barrier((parts, frame))
    frames = [frame, *bring(frame, sections, 8, 3)]
    query, keyval = combine(parts)
    first, sent = attend(False, row_lengths, x, query, exchange(keyval, ring_y), segments, frames)

    blocks = []
    for d in range(SIDE):
        route = [(number((s - 1) % sections, a - d, b, s), number(s, a, b, s)) for s, a, b in grid]
        blocks.append(lax.ppermute(sent, AXES, route))
    query, keyval = combine(exchange(project(True, blocks, [gains], weights), ring_b))
    second = attend(True, row_lengths, blocks[0], query, exchange(keyval, ring_y), segments, [])
    return first[None], second[None]


def solution(mesh):
    return jax.shard_map(
        per_device,
        mesh=mesh,
        in_specs=(
            P("section", None, "tensor"),
            P("section", "tensor"),
            P("section", None, "tensor"),
            P("section", "tensor", None),
            P(),
            P("section", None, "tensor"),
            P(),
            P(),
        ),
        out_specs=(P("section", None, "tensor"), P("section", None, "tensor")),
        check_vma=False,
    )
```

```python
import functools

import jax
import jax.numpy as jnp
from jax import lax
from jax.experimental import pallas as pl
from jax.experimental.pallas import tpu as pltpu
from jax.sharding import PartitionSpec as P

D = 4096
HEAD_DIM = 128
SIDE = 4
BLOCK = 256
KV_ROWS = 64
TOKENS = 512
HALF = 256
ROW_MAX = 128
HOST_ROWS = 2
SLOTS = 32
SENT_ROWS = TOKENS + 2 * KV_ROWS + 16
AXES = ("section", "tensor")
norm_eps = 1e-05
masked_score = -1e30
f32, bf16 = jnp.float32, jnp.bfloat16
VMEM = pl.BlockSpec(memory_space=pltpu.VMEM)
ANY = pl.BlockSpec(memory_space=pl.ANY)
SMEM = pl.BlockSpec(memory_space=pltpu.SMEM)
NT = (((1,), (1,)), ((), ()))


def place(section, first, second):
    return SIDE * first + second if section % 2 == 0 else SIDE * second + first


def rings(sections, along_a):
    groups = []
    for s in range(sections):
        for i in range(SIDE):
            ring = [(place(s, j, i) if along_a else place(s, i, j)) for j in range(SIDE)]
            groups.append([s * SIDE * SIDE + t for t in ring])
    return groups


def head_rings(sections):
    return [[(s * SIDE + g) * SIDE + i for i in range(SIDE)] for s in range(sections) for g in range(SIDE)]


def call(body, out_shape, operands, specs, flops, moved, **more):
    return pl.pallas_call(
        body,
        out_shape=out_shape,
        in_specs=specs,
        out_specs=jax.tree.map(lambda _: VMEM, out_shape),
        compiler_params=pltpu.CompilerParams(vmem_limit_bytes=12 << 20),
        cost_estimate=pl.CostEstimate(flops=flops, bytes_accessed=moved, transcendentals=0),
        **more,
    )(*operands)


def prepare_body(x_ref, gain_ref, query_ref, keyval_ref, packed_ref, own_ref, packed, own, sems):
    odd = lax.axis_index("section") % 2
    arrivals = []
    for i in range(SIDE):
        for j in range(SIDE):
            start = pl.multiple_of(jnp.where(odd == 1, SIDE * i + j, SIDE * j + i) * BLOCK, BLOCK)
            arrivals.append((query_ref.at[pl.ds(start, BLOCK)], packed.at[i, j, pl.ds(0, BLOCK)]))
            arrivals.append((keyval_ref.at[:, pl.ds(start, BLOCK)], packed.at[i, j, pl.ds(BLOCK, KV_ROWS)]))
    arrivals.append((x_ref, own.at[pl.ds(0, TOKENS)]))
    arrivals = [pltpu.make_async_copy(src, dst, sems.at[n]) for n, (src, dst) in enumerate(arrivals)]
    for copy in arrivals:
        copy.start()
    own[TOKENS:] = jnp.broadcast_to(gain_ref[...].astype(f32), (16, BLOCK)).astype(bf16)
    leaving = []
    for i in range(SIDE + 1):
        for copy in arrivals[2 * SIDE * i : 2 * SIDE * (i + 1)]:
            copy.wait()
        src, dst = (packed.at[i], packed_ref.at[i]) if i < SIDE else (own, own_ref)
        leaving.append(pltpu.make_async_copy(src, dst, sems.at[len(arrivals) + i]))
        leaving[-1].start()
    for copy in leaving:
        copy.wait()


def prepare(x, gain, w_query, w_kv):
    packed = (SIDE, SIDE, BLOCK + KV_ROWS, BLOCK)
    own = (TOKENS + 16, BLOCK)
    return pl.pallas_call(
        prepare_body,
        out_shape=(jax.ShapeDtypeStruct(packed, bf16), jax.ShapeDtypeStruct(own, bf16)),
        in_specs=[ANY, VMEM, ANY, ANY],
        out_specs=(ANY, ANY),
        scratch_shapes=[
            pltpu.VMEM(packed, bf16),
            pltpu.VMEM(own, bf16),
            pltpu.SemaphoreType.DMA((2 * SIDE * SIDE + SIDE + 2,)),
        ],
        cost_estimate=pl.CostEstimate(flops=0, bytes_accessed=6 << 20, transcendentals=0),
    )(x, gain, w_query, w_kv)


def ring_place():
    section, tensor = lax.axis_index("section"), lax.axis_index("tensor")
    return jnp.where(section % 2 == 1, tensor % SIDE, tensor // SIDE)


def project_body(is_second, *refs):
    x_refs = refs[:SIDE]
    if is_second:
        gain_ref, w_ref, out_ref, wide_ref, kv_ref = refs[SIDE:]
    else:
        w_ref, out_ref, gain_ref, wide_ref, kv_ref, held, sems = refs[SIDE:]
        copies = [pltpu.make_async_copy(ref, held.at[d], sems.at[d]) for d, ref in enumerate(x_refs)]
        for copy in copies:
            copy.start()
        x_refs = [held.at[d] for d in range(SIDE)]
    here = ring_place()
    ones = jnp.ones((8, BLOCK), bf16)
    squares = jnp.zeros((8, TOKENS), f32)
    origins = [(here + SIDE - d) % SIDE for d in range(SIDE)]
    for d in range(SIDE):
        cols = slice(d * BLOCK, (d + 1) * BLOCK)
        if not is_second:
            copies[d].wait()
            gain_ref[16 * d : 16 * (d + 1)] = x_refs[d][TOKENS:]
        part = x_refs[d][:TOKENS].astype(f32)
        wide_ref[:, cols] = (part * gain_ref[16 * d : 16 * d + 1].astype(f32)).astype(bf16)
        square = part * part
        upper = square.astype(bf16)
        lower = (square - upper.astype(f32)).astype(bf16)
        squares += lax.dot_general(ones, upper, NT, preferred_element_type=f32)
        squares += lax.dot_general(ones, lower, NT, preferred_element_type=f32)
        for b in range(SIDE):
            kv_ref[b * KV_ROWS : (b + 1) * KV_ROWS, cols] = w_ref[b, origins[d], BLOCK:]
    keyval = lax.dot_general(kv_ref[...], wide_ref[...], NT, preferred_element_type=f32).astype(bf16)
    first = squares.astype(bf16)
    second = (squares - first.astype(f32)).astype(bf16)
    stats = [first[:1, :HALF], first[:1, HALF:], second[:1, :HALF], second[:1, HALF:]]
    stats = jnp.concatenate([s.astype(f32) for s in stats] + [jnp.zeros((12, HALF), f32)], axis=0).astype(bf16)
    for b in range(SIDE):
        total = jnp.zeros((TOKENS, BLOCK), f32)
        for d in range(SIDE):
            total += jnp.dot(
                wide_ref[:, d * BLOCK : (d + 1) * BLOCK],
                w_ref[b, origins[d], :BLOCK],
                preferred_element_type=f32,
            )
        out_ref[b, :TOKENS] = total.astype(bf16)
        rows = slice(b * KV_ROWS, (b + 1) * KV_ROWS)
        out_ref[b, TOKENS : TOKENS + KV_ROWS] = keyval[rows, :HALF]
        out_ref[b, TOKENS + KV_ROWS : TOKENS + 2 * KV_ROWS] = keyval[rows, HALF:]
        out_ref[b, TOKENS + 2 * KV_ROWS :] = stats


def project(is_second, blocks, gains, weights):
    parts = jax.ShapeDtypeStruct((SIDE, SENT_ROWS, BLOCK), bf16)
    return call(
        functools.partial(project_body, is_second),
        parts if is_second else (parts, jax.ShapeDtypeStruct((16 * SIDE, BLOCK), bf16)),
        (*blocks, *gains, weights),
        [VMEM if is_second else ANY] * SIDE + [VMEM] * (len(gains) + 1),
        2 * TOKENS * 1024 * 1280,
        6 << 20,
        scratch_shapes=[
            pltpu.VMEM((TOKENS, SIDE * BLOCK), bf16),
            pltpu.VMEM((SIDE * KV_ROWS, SIDE * BLOCK), bf16),
            *([] if is_second else [pltpu.VMEM((SIDE, *blocks[0].shape), bf16), pltpu.SemaphoreType.DMA((SIDE,))]),
        ],
    )


def down(row):
    return jnp.transpose(jnp.broadcast_to(row, (HEAD_DIM, HEAD_DIM)))


def combine_body(parts_ref, query_ref, keyval_ref):
    tail = parts_ref[0, TOKENS:].astype(f32)
    for b in range(1, SIDE):
        tail += parts_ref[b, TOKENS:].astype(f32)
    stats = tail[2 * KV_ROWS :]
    for h in range(2):
        mean = (stats[h : h + 1] + stats[2 + h : 3 + h]) / D
        scale = lax.rsqrt(mean + norm_eps)
        keyval = (tail[h * KV_ROWS : (h + 1) * KV_ROWS] * scale).astype(bf16)
        for b in range(SIDE):
            keyval_ref[b, :, h * HALF : (h + 1) * HALF] = keyval
        for q in range(2):
            start = h * HALF + q * HEAD_DIM
            rows = slice(start, start + HEAD_DIM)
            total = parts_ref[0, rows].astype(f32)
            for b in range(1, SIDE):
                total += parts_ref[b, rows].astype(f32)
            factor = down(scale[:, q * HEAD_DIM : (q + 1) * HEAD_DIM])
            query_ref[rows] = (total * jnp.concatenate([factor, factor], axis=1)).astype(bf16)


def combine(parts):
    return call(
        combine_body,
        (jax.ShapeDtypeStruct((TOKENS, BLOCK), bf16), jax.ShapeDtypeStruct((SIDE, KV_ROWS, TOKENS), bf16)),
        (parts,),
        [VMEM],
        TOKENS * BLOCK * 8,
        2 << 20,
    )


def attend_body(is_second, lengths_ref, x_ref, query_ref, keyval_ref, segments_ref, *refs):
    section = lax.axis_index("section")
    if is_second:
        (out_ref,) = refs
    else:
        *frame_refs, out_ref, sent_ref, held, sems = refs
    if is_second:
        ids = segments_ref[pl.ds(jnp.maximum(section - 1, 0), 1), :]
        spot = lax.broadcasted_iota(jnp.int32, (1, TOKENS), 1)

        def count(k, carried):
            end, slot = carried
            end = end + lengths_ref[k]
            return end, slot + (spot >= end).astype(jnp.int32)

        _, slot = lax.fori_loop(0, SLOTS, count, (jnp.int32(0), jnp.zeros((1, TOKENS), jnp.int32)))
        ids = jnp.where(section == 0, slot, ids)
    else:
        ids = segments_ref[pl.ds(section, 1), :]
    ids = ids.astype(f32)
    steps = []
    for i in range(TOKENS // HEAD_DIM):
        rows = slice(i * HEAD_DIM, (i + 1) * HEAD_DIM)
        low = max(i - 1, 0) * HEAD_DIM
        width = (i + 1) * HEAD_DIM - low
        cols = slice(low, low + width)
        own = down(ids[:, rows])
        if width > HEAD_DIM:
            own = jnp.concatenate([own, own], axis=1)
        place_r = lax.broadcasted_iota(jnp.int32, (HEAD_DIM, width), 0) + i * HEAD_DIM
        place_c = lax.broadcasted_iota(jnp.int32, (HEAD_DIM, width), 1) + low
        allowed = (own == ids[:, cols]) & (place_c <= place_r)
        keys = jnp.concatenate([keyval_ref[0, :, cols], keyval_ref[1, :, cols]], axis=0)
        for h in range(2):
            lanes = slice(h * HEAD_DIM, (h + 1) * HEAD_DIM)
            scores = jnp.dot(query_ref[rows, lanes], keys, preferred_element_type=f32) * HEAD_DIM ** (-0.5)
            steps.append((rows, cols, lanes, jnp.where(allowed, scores, masked_score)))
    for n, (rows, cols, lanes, scores) in enumerate(steps):
        grown = jnp.exp(scores - jnp.max(scores, axis=1, keepdims=True))
        weights = (grown * (1.0 / jnp.sum(grown, axis=1, keepdims=True))).astype(bf16)
        steps[n] = (rows, cols, lanes, weights)
    for rows, cols, lanes, weights in steps:
        values = jnp.concatenate([keyval_ref[2, :, cols], keyval_ref[3, :, cols]], axis=0)
        context = lax.dot_general(weights, values, NT, preferred_element_type=f32).astype(bf16)
        done = (x_ref[rows, lanes].astype(f32) + context.astype(f32)).astype(bf16)
        out_ref[rows, lanes] = done
        if not is_second:
            sent_ref[rows, lanes] = done
    if not is_second:

        @pl.when(section == lax.axis_size("section") - 1)
        def _():
            copies = [pltpu.make_async_copy(ref, held.at[n], sems.at[n]) for n, ref in enumerate(frame_refs)]
            for copy in copies:
                copy.start()
            for copy in copies:
                copy.wait()
            sent_ref[...] = functools.reduce(jnp.add, [held[n].astype(f32) for n in range(SIDE)]).astype(bf16)


def attend(is_second, lengths, x, query, keyval, segments, frames):
    made = jax.ShapeDtypeStruct((TOKENS, BLOCK), bf16)
    held = pltpu.VMEM((SIDE, TOKENS, BLOCK), bf16)
    return call(
        functools.partial(attend_body, is_second),
        made if is_second else (made, made),
        (lengths, x, query, keyval, segments, *frames),
        [SMEM] + [VMEM] * 4 + [ANY] * len(frames),
        2 * TOKENS * 256 * 128 * 4,
        1 << 20,
        scratch_shapes=[] if is_second else [held, pltpu.SemaphoreType.DMA((SIDE,))],
    )


def frame_body(ids_ref, lengths_ref, pool_ref, out_ref, total_ref):
    total_ref[...] = jnp.zeros_like(total_ref)
    section = lax.axis_index("section")
    row = lax.broadcasted_iota(jnp.int32, (TOKENS, ROW_MAX), 0)
    col = lax.broadcasted_iota(jnp.int32, (TOKENS, ROW_MAX), 1)

    def take(k, start):
        length = lengths_ref[k]
        which = ids_ref[k] - HOST_ROWS * section

        @pl.when((which >= 0) & (which < HOST_ROWS))
        def _():
            hit = ((row - start == col) & (col < length)).astype(f32).astype(bf16)
            total_ref[...] += jnp.dot(hit, pool_ref[which], preferred_element_type=f32)

        return start + length

    lax.fori_loop(0, SLOTS, take, jnp.int32(0))
    out_ref[...] = total_ref[...].astype(bf16)


def make_frame(row_ids, row_lengths, pool):
    return call(
        frame_body,
        jax.ShapeDtypeStruct((TOKENS, BLOCK), bf16),
        (row_ids, row_lengths, pool),
        [SMEM, SMEM, VMEM],
        2 * TOKENS * 128 * 256,
        1 << 20,
        scratch_shapes=[pltpu.VMEM((TOKENS, BLOCK), f32)],
    )


def bring(array, sections, step, count):
    last = sections - 1
    got = []
    for n in range(1, count + 1):
        route = [(i - n * step, i) for i in range(sections) if (last - i) % ((count + 1) * step) == 0]
        got.append(lax.ppermute(array, "section", route))
    return got


def total_of(arrays):
    total = arrays[0].astype(f32)
    for array in arrays[1:]:
        total = total + array.astype(f32)
    return total.astype(bf16)


def per_device(activations, gain, w_query, w_kv, segments, pool, row_ids, row_lengths):
    sections = lax.axis_size("section")
    ring_b, ring_y = rings(sections, False), head_rings(sections)
    barrier = lax.optimization_barrier
    grid = [(s, a, b) for s in range(sections) for a in range(SIDE) for b in range(SIDE)]

    def number(s, a, b, like):
        return s * SIDE * SIDE + place(like, a % SIDE, b)

    def exchange(array, ring):
        return lax.all_to_all(array, AXES, 0, 0, axis_index_groups=ring)

    x = activations[0]
    packed, own = prepare(x, gain, w_query[0], w_kv[0])
    weights = exchange(packed, ring_b)
    blocks = [own]
    for d in range(1, SIDE):
        route = [(number(s, a - d, b, s), number(s, a, b, s)) for s, a, b in grid]
        blocks.append(lax.ppermute(own, AXES, route))

    frame = make_frame(row_ids, row_lengths, pool)
    piece = bring(frame, sections, 1, 1)[0]
    blocks[SIDE - 1], piece = barrier((blocks[SIDE - 1], piece))
    frame = frame + piece
    pieces = bring(frame, sections, 2, 3)
    weights, pieces = barrier((weights, pieces))
    frame = total_of([frame, *pieces])
    frames = [frame, *bring(frame, sections, 8, 3)]

    parts, gains = project(False, blocks, [], weights)
    parts = exchange(parts, ring_b)
    query, keyval = combine(parts)
    keyval, frames = barrier((keyval, frames))
    first, sent = attend(False, row_lengths, x, query, exchange(keyval, ring_y), segments, frames)

    blocks = []
    for d in range(SIDE):
        route = [(number((s - 1) % sections, a - d, b, s), number(s, a, b, s)) for s, a, b in grid]
        blocks.append(lax.ppermute(sent, AXES, route))
    query, keyval = combine(exchange(project(True, blocks, [gains], weights), ring_b))
    second = attend(True, row_lengths, blocks[0], query, exchange(keyval, ring_y), segments, [])
    return first[None], second[None]


def solution(mesh):
    return jax.shard_map(
        per_device,
        mesh=mesh,
        in_specs=(
            P("section", None, "tensor"),
            P("section", "tensor"),
            P("section", None, "tensor"),
            P("section", "tensor", None),
            P(),
            P("section", None, "tensor"),
            P(),
            P(),
        ),
        out_specs=(P("section", None, "tensor"), P("section", None, "tensor")),
        check_vma=False,
    )
```

```python
import functools

import jax
import jax.numpy as jnp
from jax import lax
from jax.experimental import pallas as pl
from jax.experimental.pallas import tpu as pltpu
from jax.sharding import PartitionSpec as P

D = 4096
HEAD_DIM = 128
SIDE = 4
BLOCK = 256
KV_ROWS = 64
TOKENS = 512
HALF = 256
ROW_MAX = 128
HOST_ROWS = 2
SLOTS = 32
NEAR = 8
SENT_ROWS = TOKENS + 2 * KV_ROWS + 16
AXES = ("section", "tensor")
norm_eps = 1e-05
masked_score = -1e30
f32, bf16 = jnp.float32, jnp.bfloat16
VMEM = pl.BlockSpec(memory_space=pltpu.VMEM)
ANY = pl.BlockSpec(memory_space=pl.ANY)
SMEM = pl.BlockSpec(memory_space=pltpu.SMEM)
NT = (((1,), (1,)), ((), ()))


def place(section, first, second):
    return SIDE * first + second if section % 2 == 0 else SIDE * second + first


def rings(sections, along_a):
    groups = []
    for s in range(sections):
        for i in range(SIDE):
            ring = [(place(s, j, i) if along_a else place(s, i, j)) for j in range(SIDE)]
            groups.append([s * SIDE * SIDE + t for t in ring])
    return groups


def head_rings(sections):
    return [[(s * SIDE + g) * SIDE + i for i in range(SIDE)] for s in range(sections) for g in range(SIDE)]


def call(body, out_shape, operands, specs, flops, moved, **more):
    return pl.pallas_call(
        body,
        out_shape=out_shape,
        in_specs=specs,
        out_specs=jax.tree.map(lambda _: VMEM, out_shape),
        compiler_params=pltpu.CompilerParams(vmem_limit_bytes=12 << 20),
        cost_estimate=pl.CostEstimate(flops=flops, bytes_accessed=moved, transcendentals=0),
        **more,
    )(*operands)


def prepare_body(ids_ref, x_ref, gain_ref, query_ref, keyval_ref, pool_ref, *refs):
    packed_ref, own_ref, row_ref, packed, own, row, sems = refs
    section = lax.axis_index("section")
    odd = section % 2

    def find(k, which):
        local = ids_ref[k] - HOST_ROWS * section
        return jnp.where((local >= 0) & (local < HOST_ROWS), local, which)

    which = lax.fori_loop(0, SLOTS, find, jnp.int32(0))
    arrivals = []
    for i in range(SIDE):
        for j in range(SIDE):
            start = pl.multiple_of(jnp.where(odd == 1, SIDE * i + j, SIDE * j + i) * BLOCK, BLOCK)
            arrivals.append((query_ref.at[pl.ds(start, BLOCK)], packed.at[i, j, pl.ds(0, BLOCK)]))
            arrivals.append((keyval_ref.at[:, pl.ds(start, BLOCK)], packed.at[i, j, pl.ds(BLOCK, KV_ROWS)]))
    arrivals.append((x_ref, own.at[pl.ds(0, TOKENS)]))
    arrivals.append((pool_ref.at[which], row))
    arrivals = [pltpu.make_async_copy(src, dst, sems.at[n]) for n, (src, dst) in enumerate(arrivals)]
    for copy in arrivals:
        copy.start()
    own[TOKENS:] = jnp.broadcast_to(gain_ref[...].astype(f32), (16, BLOCK)).astype(bf16)
    leaving = []
    ready = [(packed.at[i], packed_ref.at[i], arrivals[2 * SIDE * i : 2 * SIDE * (i + 1)]) for i in range(SIDE)]
    ready += [(own, own_ref, arrivals[-2:-1]), (row, row_ref, arrivals[-1:])]
    for n, (src, dst, waits) in enumerate(ready):
        for copy in waits:
            copy.wait()
        leaving.append(pltpu.make_async_copy(src, dst, sems.at[len(arrivals) + n]))
        leaving[-1].start()
    for copy in leaving:
        copy.wait()


def prepare(row_ids, x, gain, w_query, w_kv, pool):
    packed = (SIDE, SIDE, BLOCK + KV_ROWS, BLOCK)
    own = (TOKENS + 16, BLOCK)
    row = pool.shape[1:]
    return pl.pallas_call(
        prepare_body,
        out_shape=tuple(jax.ShapeDtypeStruct(shape, bf16) for shape in (packed, own, row)),
        in_specs=[SMEM, ANY, VMEM, ANY, ANY, ANY],
        out_specs=(ANY, ANY, ANY),
        scratch_shapes=[
            pltpu.VMEM(packed, bf16),
            pltpu.VMEM(own, bf16),
            pltpu.VMEM(row, bf16),
            pltpu.SemaphoreType.DMA((2 * SIDE * SIDE + SIDE + 4,)),
        ],
        cost_estimate=pl.CostEstimate(flops=0, bytes_accessed=6 << 20, transcendentals=0),
    )(row_ids, x, gain, w_query, w_kv, pool)


def ring_place():
    section, tensor = lax.axis_index("section"), lax.axis_index("tensor")
    return jnp.where(section % 2 == 1, tensor % SIDE, tensor // SIDE)


def project_body(is_second, *refs):
    x_refs = refs[:SIDE]
    if is_second:
        gain_ref, w_ref, out_ref, wide_ref, kv_ref = refs[SIDE:]
    else:
        w_ref, out_ref, gain_ref, wide_ref, kv_ref, held, sems = refs[SIDE:]
        copies = [pltpu.make_async_copy(ref, held.at[d], sems.at[d]) for d, ref in enumerate(x_refs)]
        for copy in copies:
            copy.start()
        x_refs = [held.at[d] for d in range(SIDE)]
    here = ring_place()
    ones = jnp.ones((8, BLOCK), bf16)
    squares = jnp.zeros((8, TOKENS), f32)
    origins = [(here + SIDE - d) % SIDE for d in range(SIDE)]
    for d in range(SIDE):
        cols = slice(d * BLOCK, (d + 1) * BLOCK)
        if not is_second:
            copies[d].wait()
            gain_ref[16 * d : 16 * (d + 1)] = x_refs[d][TOKENS:]
        part = x_refs[d][:TOKENS].astype(f32)
        wide_ref[:, cols] = (part * gain_ref[16 * d : 16 * d + 1].astype(f32)).astype(bf16)
        square = part * part
        upper = square.astype(bf16)
        lower = (square - upper.astype(f32)).astype(bf16)
        squares += lax.dot_general(ones, upper, NT, preferred_element_type=f32)
        squares += lax.dot_general(ones, lower, NT, preferred_element_type=f32)
        for b in range(SIDE):
            kv_ref[b * KV_ROWS : (b + 1) * KV_ROWS, cols] = w_ref[b, origins[d], BLOCK:]
    keyval = lax.dot_general(kv_ref[...], wide_ref[...], NT, preferred_element_type=f32).astype(bf16)
    first = squares.astype(bf16)
    second = (squares - first.astype(f32)).astype(bf16)
    stats = [first[:1, :HALF], first[:1, HALF:], second[:1, :HALF], second[:1, HALF:]]
    stats = jnp.concatenate([s.astype(f32) for s in stats] + [jnp.zeros((12, HALF), f32)], axis=0).astype(bf16)
    for b in range(SIDE):
        total = jnp.zeros((TOKENS, BLOCK), f32)
        for d in range(SIDE):
            total += jnp.dot(
                wide_ref[:, d * BLOCK : (d + 1) * BLOCK],
                w_ref[b, origins[d], :BLOCK],
                preferred_element_type=f32,
            )
        out_ref[b, :TOKENS] = total.astype(bf16)
        rows = slice(b * KV_ROWS, (b + 1) * KV_ROWS)
        out_ref[b, TOKENS : TOKENS + KV_ROWS] = keyval[rows, :HALF]
        out_ref[b, TOKENS + KV_ROWS : TOKENS + 2 * KV_ROWS] = keyval[rows, HALF:]
        out_ref[b, TOKENS + 2 * KV_ROWS :] = stats


def project(is_second, blocks, gains, weights):
    parts = jax.ShapeDtypeStruct((SIDE, SENT_ROWS, BLOCK), bf16)
    return call(
        functools.partial(project_body, is_second),
        parts if is_second else (parts, jax.ShapeDtypeStruct((16 * SIDE, BLOCK), bf16)),
        (*blocks, *gains, weights),
        [VMEM if is_second else ANY] * SIDE + [VMEM] * (len(gains) + 1),
        2 * TOKENS * 1024 * 1280,
        6 << 20,
        scratch_shapes=[
            pltpu.VMEM((TOKENS, SIDE * BLOCK), bf16),
            pltpu.VMEM((SIDE * KV_ROWS, SIDE * BLOCK), bf16),
            *([] if is_second else [pltpu.VMEM((SIDE, *blocks[0].shape), bf16), pltpu.SemaphoreType.DMA((SIDE,))]),
        ],
    )


def down(row):
    return jnp.transpose(jnp.broadcast_to(row, (HEAD_DIM, HEAD_DIM)))


def combine_body(parts_ref, query_ref, keyval_ref):
    tail = parts_ref[0, TOKENS:].astype(f32)
    for b in range(1, SIDE):
        tail += parts_ref[b, TOKENS:].astype(f32)
    stats = tail[2 * KV_ROWS :]
    for h in range(2):
        mean = (stats[h : h + 1] + stats[2 + h : 3 + h]) / D
        scale = lax.rsqrt(mean + norm_eps)
        keyval = (tail[h * KV_ROWS : (h + 1) * KV_ROWS] * scale).astype(bf16)
        for b in range(SIDE):
            keyval_ref[b, :, h * HALF : (h + 1) * HALF] = keyval
        for q in range(2):
            start = h * HALF + q * HEAD_DIM
            rows = slice(start, start + HEAD_DIM)
            total = parts_ref[0, rows].astype(f32)
            for b in range(1, SIDE):
                total += parts_ref[b, rows].astype(f32)
            factor = down(scale[:, q * HEAD_DIM : (q + 1) * HEAD_DIM])
            query_ref[rows] = (total * jnp.concatenate([factor, factor], axis=1)).astype(bf16)


def combine(parts):
    return call(
        combine_body,
        (jax.ShapeDtypeStruct((TOKENS, BLOCK), bf16), jax.ShapeDtypeStruct((SIDE, KV_ROWS, TOKENS), bf16)),
        (parts,),
        [VMEM],
        TOKENS * BLOCK * 8,
        2 << 20,
    )


def attend_body(is_second, lengths_ref, x_ref, query_ref, keyval_ref, segments_ref, *refs):
    section = lax.axis_index("section")
    if is_second:
        (out_ref,) = refs
    else:
        *frame_refs, out_ref, sent_ref, held, sems = refs
    if is_second:
        ids = segments_ref[pl.ds(jnp.maximum(section - 1, 0), 1), :]
        spot = lax.broadcasted_iota(jnp.int32, (1, TOKENS), 1)

        def count(k, carried):
            end, slot = carried
            end = end + lengths_ref[k]
            return end, slot + (spot >= end).astype(jnp.int32)

        _, slot = lax.fori_loop(0, SLOTS, count, (jnp.int32(0), jnp.zeros((1, TOKENS), jnp.int32)))
        ids = jnp.where(section == 0, slot, ids)
    else:
        ids = segments_ref[pl.ds(section, 1), :]
    ids = ids.astype(f32)
    steps = []
    for i in range(TOKENS // HEAD_DIM):
        rows = slice(i * HEAD_DIM, (i + 1) * HEAD_DIM)
        low = max(i - 1, 0) * HEAD_DIM
        width = (i + 1) * HEAD_DIM - low
        cols = slice(low, low + width)
        own = down(ids[:, rows])
        if width > HEAD_DIM:
            own = jnp.concatenate([own, own], axis=1)
        place_r = lax.broadcasted_iota(jnp.int32, (HEAD_DIM, width), 0) + i * HEAD_DIM
        place_c = lax.broadcasted_iota(jnp.int32, (HEAD_DIM, width), 1) + low
        allowed = (own == ids[:, cols]) & (place_c <= place_r)
        keys = jnp.concatenate([keyval_ref[0, :, cols], keyval_ref[1, :, cols]], axis=0)
        for h in range(2):
            lanes = slice(h * HEAD_DIM, (h + 1) * HEAD_DIM)
            scores = jnp.dot(query_ref[rows, lanes], keys, preferred_element_type=f32) * HEAD_DIM ** (-0.5)
            steps.append((rows, cols, lanes, jnp.where(allowed, scores, masked_score)))
    for n, (rows, cols, lanes, scores) in enumerate(steps):
        grown = jnp.exp(scores - jnp.max(scores, axis=1, keepdims=True))
        weights = (grown * (1.0 / jnp.sum(grown, axis=1, keepdims=True))).astype(bf16)
        steps[n] = (rows, cols, lanes, weights)
    for rows, cols, lanes, weights in steps:
        values = jnp.concatenate([keyval_ref[2, :, cols], keyval_ref[3, :, cols]], axis=0)
        context = lax.dot_general(weights, values, NT, preferred_element_type=f32).astype(bf16)
        done = (x_ref[rows, lanes].astype(f32) + context.astype(f32)).astype(bf16)
        out_ref[rows, lanes] = done
        if not is_second:
            sent_ref[rows, lanes] = done
    if not is_second:

        @pl.when(section == lax.axis_size("section") - 1)
        def _():
            copies = [pltpu.make_async_copy(ref, held.at[n], sems.at[n]) for n, ref in enumerate(frame_refs)]
            for copy in copies:
                copy.start()
            for copy in copies:
                copy.wait()
            sent_ref[...] = functools.reduce(jnp.add, [held[n].astype(f32) for n in range(SIDE)]).astype(bf16)


def attend(is_second, lengths, x, query, keyval, segments, frames):
    made = jax.ShapeDtypeStruct((TOKENS, BLOCK), bf16)
    held = pltpu.VMEM((SIDE, TOKENS, BLOCK), bf16)
    return call(
        functools.partial(attend_body, is_second),
        made if is_second else (made, made),
        (lengths, x, query, keyval, segments, *frames),
        [SMEM] + [VMEM] * 4 + [ANY] * len(frames),
        2 * TOKENS * 256 * 128 * 4,
        1 << 20,
        scratch_shapes=[] if is_second else [held, pltpu.SemaphoreType.DMA((SIDE,))],
    )


def frame_body(ids_ref, lengths_ref, rows_ref, out_ref, starts, counts, hits_ref):
    base = lax.div(lax.axis_index("section"), NEAR) * NEAR
    for n in range(NEAR):
        starts[n] = 0
        counts[n] = 0

    def note(k, start):
        length = lengths_ref[k]
        host = lax.div(ids_ref[k], HOST_ROWS) - base

        @pl.when((host >= 0) & (host < NEAR))
        def _():
            starts[host] = start
            counts[host] = length

        return start + length

    lax.fori_loop(0, SLOTS, note, jnp.int32(0))
    offset = lax.broadcasted_iota(jnp.int32, (TOKENS, ROW_MAX), 0) - lax.broadcasted_iota(
        jnp.int32, (TOKENS, ROW_MAX), 1
    )
    col = lax.broadcasted_iota(jnp.int32, (TOKENS, ROW_MAX), 1)
    for n in range(NEAR):
        hit = (offset == starts[n]) & (col < counts[n])
        hits_ref[:, n * ROW_MAX : (n + 1) * ROW_MAX] = hit.astype(f32).astype(bf16)
    out_ref[...] = jnp.dot(hits_ref[...], rows_ref[...], preferred_element_type=f32).astype(bf16)


def make_frame(row_ids, row_lengths, rows):
    return call(
        frame_body,
        jax.ShapeDtypeStruct((TOKENS, BLOCK), bf16),
        (row_ids, row_lengths, rows),
        [SMEM, SMEM, VMEM],
        2 * TOKENS * NEAR * 128 * 256,
        1 << 20,
        scratch_shapes=[
            pltpu.SMEM((NEAR,), jnp.int32),
            pltpu.SMEM((NEAR,), jnp.int32),
            pltpu.VMEM((TOKENS, NEAR * ROW_MAX), bf16),
        ],
    )


def per_device(activations, gain, w_query, w_kv, segments, pool, row_ids, row_lengths):
    sections = lax.axis_size("section")
    ring_b, ring_y = rings(sections, False), head_rings(sections)
    barrier = lax.optimization_barrier
    grid = [(s, a, b) for s in range(sections) for a in range(SIDE) for b in range(SIDE)]

    def number(s, a, b, like):
        return s * SIDE * SIDE + place(like, a % SIDE, b)

    def exchange(array, ring):
        return lax.all_to_all(array, AXES, 0, 0, axis_index_groups=ring)

    x = activations[0]
    packed, own, row = prepare(row_ids, x, gain, w_query[0], w_kv[0], pool)
    weights = exchange(packed, ring_b)
    blocks = [own]
    for d in range(1, SIDE):
        route = [(number(s, a - d, b, s), number(s, a, b, s)) for s, a, b in grid]
        blocks.append(lax.ppermute(own, AXES, route))

    tensors = range(SIDE * SIDE)
    pairs = [[(s + c) * SIDE * SIDE + t for c in range(2)] for s in range(0, sections, 2) for t in tensors]
    fours = [
        [(s + c + 2 * z) * SIDE * SIDE + t for z in range(NEAR // 2)]
        for s in range(0, sections, NEAR)
        for c in range(2)
        for t in tensors
    ]
    rows = lax.all_gather(row, AXES, axis=0, axis_index_groups=pairs, tiled=True)
    rows = lax.all_gather(rows, AXES, axis=0, axis_index_groups=fours, tiled=True)
    frame = make_frame(row_ids, row_lengths, rows)
    weights, frame = barrier((weights, frame))
    last = sections - 1
    sources = [1 if n == 0 else (n * NEAR + 1 if 2 * n < sections // NEAR else n * NEAR + NEAR - 1) for n in range(last // NEAR)]
    frames = [frame, *[lax.ppermute(frame, "section", [(source, last)]) for source in sources]]

    parts, gains = project(False, blocks, [], weights)
    parts = exchange(parts, ring_b)
    query, keyval = combine(parts)
    keyval, frames = barrier((keyval, frames))
    first, sent = attend(False, row_lengths, x, query, exchange(keyval, ring_y), segments, frames)

    blocks = []
    for d in range(SIDE):
        route = [(number((s - 1) % sections, a - d, b, s), number(s, a, b, s)) for s, a, b in grid]
        blocks.append(lax.ppermute(sent, AXES, route))
    query, keyval = combine(exchange(project(True, blocks, [gains], weights), ring_b))
    second = attend(True, row_lengths, blocks[0], query, exchange(keyval, ring_y), segments, [])
    return first[None], second[None]


def solution(mesh):
    return jax.shard_map(
        per_device,
        mesh=mesh,
        in_specs=(
            P("section", None, "tensor"),
            P("section", "tensor"),
            P("section", None, "tensor"),
            P("section", "tensor", None),
            P(),
            P("section", None, "tensor"),
            P(),
            P(),
        ),
        out_specs=(P("section", None, "tensor"), P("section", None, "tensor")),
        check_vma=False,
    )
```

```python
import functools

import jax
import jax.numpy as jnp
from jax import lax
from jax.experimental import pallas as pl
from jax.experimental.pallas import tpu as pltpu
from jax.sharding import PartitionSpec as P

D = 4096
HEAD_DIM = 128
SIDE = 4
BLOCK = 256
KV_ROWS = 64
TOKENS = 512
HALF = 256
ROW_MAX = 128
HOST_ROWS = 2
SLOTS = 32
NEAR = 8
SENT_ROWS = TOKENS + 2 * KV_ROWS + 16
AXES = ("section", "tensor")
norm_eps = 1e-05
masked_score = -1e30
f32, bf16 = jnp.float32, jnp.bfloat16
VMEM = pl.BlockSpec(memory_space=pltpu.VMEM)
ANY = pl.BlockSpec(memory_space=pl.ANY)
SMEM = pl.BlockSpec(memory_space=pltpu.SMEM)
NT = (((1,), (1,)), ((), ()))


def place(section, first, second):
    return SIDE * first + second if section % 2 == 0 else SIDE * second + first


def rings(sections, along_a):
    groups = []
    for s in range(sections):
        for i in range(SIDE):
            ring = [(place(s, j, i) if along_a else place(s, i, j)) for j in range(SIDE)]
            groups.append([s * SIDE * SIDE + t for t in ring])
    return groups


def head_rings(sections):
    return [[(s * SIDE + g) * SIDE + i for i in range(SIDE)] for s in range(sections) for g in range(SIDE)]


def call(body, out_shape, operands, specs, flops, moved, **more):
    return pl.pallas_call(
        body,
        out_shape=out_shape,
        in_specs=specs,
        out_specs=jax.tree.map(lambda _: VMEM, out_shape),
        compiler_params=pltpu.CompilerParams(vmem_limit_bytes=12 << 20),
        cost_estimate=pl.CostEstimate(flops=flops, bytes_accessed=moved, transcendentals=0),
        **more,
    )(*operands)


def prepare_body(ids_ref, x_ref, gain_ref, query_ref, keyval_ref, pool_ref, *refs):
    packed_ref, own_ref, row_ref, packed, own, row, sems = refs
    section = lax.axis_index("section")
    odd = section % 2

    def find(k, which):
        local = ids_ref[k] - HOST_ROWS * section
        return jnp.where((local >= 0) & (local < HOST_ROWS), local, which)

    which = lax.fori_loop(0, SLOTS, find, jnp.int32(0))
    arrivals = []
    for i in range(SIDE):
        for j in range(SIDE):
            start = pl.multiple_of(jnp.where(odd == 1, SIDE * i + j, SIDE * j + i) * BLOCK, BLOCK)
            arrivals.append((query_ref.at[pl.ds(start, BLOCK)], packed.at[i, j, pl.ds(0, BLOCK)]))
            arrivals.append((keyval_ref.at[:, pl.ds(start, BLOCK)], packed.at[i, j, pl.ds(BLOCK, KV_ROWS)]))
    arrivals.append((x_ref, own.at[pl.ds(0, TOKENS)]))
    arrivals.append((pool_ref.at[which], row))
    arrivals = [pltpu.make_async_copy(src, dst, sems.at[n]) for n, (src, dst) in enumerate(arrivals)]
    for copy in arrivals:
        copy.start()
    own[TOKENS:] = jnp.broadcast_to(gain_ref[...].astype(f32), (16, BLOCK)).astype(bf16)
    leaving = []
    ready = [(packed.at[i], packed_ref.at[i], arrivals[2 * SIDE * i : 2 * SIDE * (i + 1)]) for i in range(SIDE)]
    ready += [(own, own_ref, arrivals[-2:-1]), (row, row_ref, arrivals[-1:])]
    for n, (src, dst, waits) in enumerate(ready):
        for copy in waits:
            copy.wait()
        leaving.append(pltpu.make_async_copy(src, dst, sems.at[len(arrivals) + n]))
        leaving[-1].start()
    for copy in leaving:
        copy.wait()


def prepare(row_ids, x, gain, w_query, w_kv, pool):
    packed = (SIDE, SIDE, BLOCK + KV_ROWS, BLOCK)
    own = (TOKENS + 16, BLOCK)
    row = pool.shape[1:]
    return pl.pallas_call(
        prepare_body,
        out_shape=tuple(jax.ShapeDtypeStruct(shape, bf16) for shape in (packed, own, row)),
        in_specs=[SMEM, ANY, VMEM, ANY, ANY, ANY],
        out_specs=(ANY, ANY, ANY),
        scratch_shapes=[
            pltpu.VMEM(packed, bf16),
            pltpu.VMEM(own, bf16),
            pltpu.VMEM(row, bf16),
            pltpu.SemaphoreType.DMA((2 * SIDE * SIDE + SIDE + 4,)),
        ],
        cost_estimate=pl.CostEstimate(flops=0, bytes_accessed=6 << 20, transcendentals=0),
    )(row_ids, x, gain, w_query, w_kv, pool)


def ring_place():
    section, tensor = lax.axis_index("section"), lax.axis_index("tensor")
    return jnp.where(section % 2 == 1, tensor % SIDE, tensor // SIDE)


def project_body(is_second, *refs):
    x_refs = refs[:SIDE]
    if is_second:
        gain_ref, w_ref, out_ref, wide_ref, kv_ref = refs[SIDE:]
    else:
        w_ref, out_ref, gain_ref, wide_ref, kv_ref, held, sems = refs[SIDE:]
        copies = [pltpu.make_async_copy(ref, held.at[d], sems.at[d]) for d, ref in enumerate(x_refs)]
        for copy in copies:
            copy.start()
        x_refs = [held.at[d] for d in range(SIDE)]
    here = ring_place()
    ones = jnp.ones((8, BLOCK), bf16)
    squares = jnp.zeros((8, TOKENS), f32)
    origins = [(here + SIDE - d) % SIDE for d in range(SIDE)]
    for d in range(SIDE):
        cols = slice(d * BLOCK, (d + 1) * BLOCK)
        if not is_second:
            copies[d].wait()
            gain_ref[16 * d : 16 * (d + 1)] = x_refs[d][TOKENS:]
        part = x_refs[d][:TOKENS].astype(f32)
        wide_ref[:, cols] = (part * gain_ref[16 * d : 16 * d + 1].astype(f32)).astype(bf16)
        square = part * part
        upper = square.astype(bf16)
        lower = (square - upper.astype(f32)).astype(bf16)
        squares += lax.dot_general(ones, upper, NT, preferred_element_type=f32)
        squares += lax.dot_general(ones, lower, NT, preferred_element_type=f32)
        for b in range(SIDE):
            kv_ref[b * KV_ROWS : (b + 1) * KV_ROWS, cols] = w_ref[b, origins[d], BLOCK:]
    keyval = lax.dot_general(kv_ref[...], wide_ref[...], NT, preferred_element_type=f32).astype(bf16)
    first = squares.astype(bf16)
    second = (squares - first.astype(f32)).astype(bf16)
    stats = [first[:1, :HALF], first[:1, HALF:], second[:1, :HALF], second[:1, HALF:]]
    stats = jnp.concatenate([s.astype(f32) for s in stats] + [jnp.zeros((12, HALF), f32)], axis=0).astype(bf16)
    for b in range(SIDE):
        total = jnp.zeros((TOKENS, BLOCK), f32)
        for d in range(SIDE):
            total += jnp.dot(
                wide_ref[:, d * BLOCK : (d + 1) * BLOCK],
                w_ref[b, origins[d], :BLOCK],
                preferred_element_type=f32,
            )
        out_ref[b, :TOKENS] = total.astype(bf16)
        rows = slice(b * KV_ROWS, (b + 1) * KV_ROWS)
        out_ref[b, TOKENS : TOKENS + KV_ROWS] = keyval[rows, :HALF]
        out_ref[b, TOKENS + KV_ROWS : TOKENS + 2 * KV_ROWS] = keyval[rows, HALF:]
        out_ref[b, TOKENS + 2 * KV_ROWS :] = stats


def project(is_second, blocks, gains, weights):
    parts = jax.ShapeDtypeStruct((SIDE, SENT_ROWS, BLOCK), bf16)
    return call(
        functools.partial(project_body, is_second),
        parts if is_second else (parts, jax.ShapeDtypeStruct((16 * SIDE, BLOCK), bf16)),
        (*blocks, *gains, weights),
        [VMEM if is_second else ANY] * SIDE + [VMEM] * (len(gains) + 1),
        2 * TOKENS * 1024 * 1280,
        6 << 20,
        scratch_shapes=[
            pltpu.VMEM((TOKENS, SIDE * BLOCK), bf16),
            pltpu.VMEM((SIDE * KV_ROWS, SIDE * BLOCK), bf16),
            *([] if is_second else [pltpu.VMEM((SIDE, *blocks[0].shape), bf16), pltpu.SemaphoreType.DMA((SIDE,))]),
        ],
    )


def down(row):
    return jnp.transpose(jnp.broadcast_to(row, (HEAD_DIM, HEAD_DIM)))


def combine_body(parts_ref, query_ref, keyval_ref):
    tail = parts_ref[0, TOKENS:].astype(f32)
    for b in range(1, SIDE):
        tail += parts_ref[b, TOKENS:].astype(f32)
    stats = tail[2 * KV_ROWS :]
    for h in range(2):
        mean = (stats[h : h + 1] + stats[2 + h : 3 + h]) / D
        scale = lax.rsqrt(mean + norm_eps)
        keyval = (tail[h * KV_ROWS : (h + 1) * KV_ROWS] * scale).astype(bf16)
        for b in range(SIDE):
            keyval_ref[b, :, h * HALF : (h + 1) * HALF] = keyval
        for q in range(2):
            start = h * HALF + q * HEAD_DIM
            rows = slice(start, start + HEAD_DIM)
            total = parts_ref[0, rows].astype(f32)
            for b in range(1, SIDE):
                total += parts_ref[b, rows].astype(f32)
            factor = down(scale[:, q * HEAD_DIM : (q + 1) * HEAD_DIM])
            query_ref[rows] = (total * jnp.concatenate([factor, factor], axis=1)).astype(bf16)


def combine(parts):
    return call(
        combine_body,
        (jax.ShapeDtypeStruct((TOKENS, BLOCK), bf16), jax.ShapeDtypeStruct((SIDE, KV_ROWS, TOKENS), bf16)),
        (parts,),
        [VMEM],
        TOKENS * BLOCK * 8,
        2 << 20,
    )


def attend_body(is_second, lengths_ref, x_ref, query_ref, keyval_ref, segments_ref, *refs):
    section = lax.axis_index("section")
    if is_second:
        (out_ref,) = refs
    else:
        *frame_refs, out_ref, sent_ref, held, sems = refs
    if is_second:
        ids = segments_ref[pl.ds(jnp.maximum(section - 1, 0), 1), :]
        spot = lax.broadcasted_iota(jnp.int32, (1, TOKENS), 1)

        def count(k, carried):
            end, slot = carried
            end = end + lengths_ref[k]
            return end, slot + (spot >= end).astype(jnp.int32)

        _, slot = lax.fori_loop(0, SLOTS, count, (jnp.int32(0), jnp.zeros((1, TOKENS), jnp.int32)))
        ids = jnp.where(section == 0, slot, ids)
    else:
        ids = segments_ref[pl.ds(section, 1), :]
    ids = ids.astype(f32)
    steps = []
    for i in range(TOKENS // HEAD_DIM):
        rows = slice(i * HEAD_DIM, (i + 1) * HEAD_DIM)
        low = max(i - 1, 0) * HEAD_DIM
        width = (i + 1) * HEAD_DIM - low
        cols = slice(low, low + width)
        own = down(ids[:, rows])
        if width > HEAD_DIM:
            own = jnp.concatenate([own, own], axis=1)
        place_r = lax.broadcasted_iota(jnp.int32, (HEAD_DIM, width), 0) + i * HEAD_DIM
        place_c = lax.broadcasted_iota(jnp.int32, (HEAD_DIM, width), 1) + low
        allowed = (own == ids[:, cols]) & (place_c <= place_r)
        keys = jnp.concatenate([keyval_ref[0, :, cols], keyval_ref[1, :, cols]], axis=0)
        for h in range(2):
            lanes = slice(h * HEAD_DIM, (h + 1) * HEAD_DIM)
            scores = jnp.dot(query_ref[rows, lanes], keys, preferred_element_type=f32) * HEAD_DIM ** (-0.5)
            steps.append((rows, cols, lanes, jnp.where(allowed, scores, masked_score)))
    for n, (rows, cols, lanes, scores) in enumerate(steps):
        grown = jnp.exp(scores - jnp.max(scores, axis=1, keepdims=True))
        weights = (grown * (1.0 / jnp.sum(grown, axis=1, keepdims=True))).astype(bf16)
        steps[n] = (rows, cols, lanes, weights)
    for rows, cols, lanes, weights in steps:
        values = jnp.concatenate([keyval_ref[2, :, cols], keyval_ref[3, :, cols]], axis=0)
        context = lax.dot_general(weights, values, NT, preferred_element_type=f32).astype(bf16)
        done = (x_ref[rows, lanes].astype(f32) + context.astype(f32)).astype(bf16)
        out_ref[rows, lanes] = done
        if not is_second:
            sent_ref[rows, lanes] = done
    if not is_second:

        @pl.when(section == lax.axis_size("section") - 1)
        def _():
            copies = [pltpu.make_async_copy(ref, held.at[n], sems.at[n]) for n, ref in enumerate(frame_refs)]
            for copy in copies:
                copy.start()
            for copy in copies:
                copy.wait()
            sent_ref[...] = functools.reduce(jnp.add, [held[n].astype(f32) for n in range(SIDE)]).astype(bf16)


def attend(is_second, lengths, x, query, keyval, segments, frames):
    made = jax.ShapeDtypeStruct((TOKENS, BLOCK), bf16)
    held = pltpu.VMEM((SIDE, TOKENS, BLOCK), bf16)
    return call(
        functools.partial(attend_body, is_second),
        made if is_second else (made, made),
        (lengths, x, query, keyval, segments, *frames),
        [SMEM] + [VMEM] * 4 + [ANY] * len(frames),
        2 * TOKENS * 256 * 128 * 4,
        1 << 20,
        scratch_shapes=[] if is_second else [held, pltpu.SemaphoreType.DMA((SIDE,))],
    )


def frame_body(ids_ref, lengths_ref, *refs):
    pair_refs, (out_ref, starts, counts, rows_ref, hits_ref) = refs[: NEAR // 2], refs[NEAR // 2 :]
    section = lax.axis_index("section")
    for n in range(NEAR):
        starts[n] = 0
        counts[n] = 0
    for n, ref in enumerate(pair_refs):
        rows_ref[2 * n * ROW_MAX : 2 * (n + 1) * ROW_MAX] = ref[...]

    def note(k, start):
        length = lengths_ref[k]
        behind = section - lax.div(ids_ref[k], HOST_ROWS)

        @pl.when((behind >= 0) & (behind < NEAR))
        def _():
            spot = behind + 1 - 2 * (behind % 2)
            starts[spot] = start
            counts[spot] = length

        return start + length

    lax.fori_loop(0, SLOTS, note, jnp.int32(0))
    offset = lax.broadcasted_iota(jnp.int32, (TOKENS, ROW_MAX), 0) - lax.broadcasted_iota(
        jnp.int32, (TOKENS, ROW_MAX), 1
    )
    col = lax.broadcasted_iota(jnp.int32, (TOKENS, ROW_MAX), 1)
    for n in range(NEAR):
        hit = (offset == starts[n]) & (col < counts[n])
        hits_ref[:, n * ROW_MAX : (n + 1) * ROW_MAX] = hit.astype(f32).astype(bf16)
    out_ref[...] = jnp.dot(hits_ref[...], rows_ref[...], preferred_element_type=f32).astype(bf16)


def make_frame(row_ids, row_lengths, rows):
    return call(
        frame_body,
        jax.ShapeDtypeStruct((TOKENS, BLOCK), bf16),
        (row_ids, row_lengths, *rows),
        [SMEM, SMEM] + [VMEM] * (NEAR // 2),
        2 * TOKENS * NEAR * 128 * 256,
        1 << 20,
        scratch_shapes=[
            pltpu.SMEM((NEAR,), jnp.int32),
            pltpu.SMEM((NEAR,), jnp.int32),
            pltpu.VMEM((NEAR * ROW_MAX, BLOCK), bf16),
            pltpu.VMEM((TOKENS, NEAR * ROW_MAX), bf16),
        ],
    )


def bring(array, sections, step, count):
    last, span = sections - 1, (count + 1) * step
    got = []
    for n in range(1, count + 1):
        route = [(i - n * step, i) for i in range(sections) if (last - i) % span == 0]
        got.append(lax.ppermute(array, "section", route))
    return got


def per_device(activations, gain, w_query, w_kv, segments, pool, row_ids, row_lengths):
    sections = lax.axis_size("section")
    ring_b, ring_y = rings(sections, False), head_rings(sections)
    barrier = lax.optimization_barrier
    grid = [(s, a, b) for s in range(sections) for a in range(SIDE) for b in range(SIDE)]

    def number(s, a, b, like):
        return s * SIDE * SIDE + place(like, a % SIDE, b)

    def exchange(array, ring):
        return lax.all_to_all(array, AXES, 0, 0, axis_index_groups=ring)

    x = activations[0]
    packed, own, row = prepare(row_ids, x, gain, w_query[0], w_kv[0], pool)
    weights = exchange(packed, ring_b)
    blocks = [own]
    for d in range(1, SIDE):
        route = [(number(s, a - d, b, s), number(s, a, b, s)) for s, a, b in grid]
        blocks.append(lax.ppermute(own, AXES, route))

    pair = jnp.concatenate([*bring(row, sections, 1, 1), row], axis=0)
    blocks[SIDE - 1], pair = barrier((blocks[SIDE - 1], pair))
    pairs = [pair, *bring(pair, sections, 2, NEAR // 2 - 1)]
    frame = make_frame(row_ids, row_lengths, pairs)
    weights, frame = barrier((weights, frame))
    frames = [frame, *bring(frame, sections, NEAR, sections // NEAR - 1)]

    parts, gains = project(False, blocks, [], weights)
    parts = exchange(parts, ring_b)
    query, keyval = combine(parts)
    keyval, frames = barrier((keyval, frames))
    first, sent = attend(False, row_lengths, x, query, exchange(keyval, ring_y), segments, frames)

    blocks = []
    for d in range(SIDE):
        route = [(number((s - 1) % sections, a - d, b, s), number(s, a, b, s)) for s, a, b in grid]
        blocks.append(lax.ppermute(sent, AXES, route))
    query, keyval = combine(exchange(project(True, blocks, [gains], weights), ring_b))
    second = attend(True, row_lengths, blocks[0], query, exchange(keyval, ring_y), segments, [])
    return first[None], second[None]


def solution(mesh):
    return jax.shard_map(
        per_device,
        mesh=mesh,
        in_specs=(
            P("section", None, "tensor"),
            P("section", "tensor"),
            P("section", None, "tensor"),
            P("section", "tensor", None),
            P(),
            P("section", None, "tensor"),
            P(),
            P(),
        ),
        out_specs=(P("section", None, "tensor"), P("section", None, "tensor")),
        check_vma=False,
    )
```

```python
import functools

import jax
import jax.numpy as jnp
from jax import lax
from jax.experimental import pallas as pl
from jax.experimental.pallas import tpu as pltpu
from jax.sharding import PartitionSpec as P

D = 4096
HEAD_DIM = 128
SIDE = 4
BLOCK = 256
KV_ROWS = 64
TOKENS = 512
HALF = 256
ROW_MAX = 128
HOST_ROWS = 2
SLOTS = 32
NEAR = 8
SENT_ROWS = TOKENS + 2 * KV_ROWS + 16
AXES = ("section", "tensor")
norm_eps = 1e-05
masked_score = -1e30
f32, bf16 = jnp.float32, jnp.bfloat16
VMEM = pl.BlockSpec(memory_space=pltpu.VMEM)
ANY = pl.BlockSpec(memory_space=pl.ANY)
SMEM = pl.BlockSpec(memory_space=pltpu.SMEM)
NT = (((1,), (1,)), ((), ()))


def place(section, first, second):
    return SIDE * first + second if section % 2 == 0 else SIDE * second + first


def rings(sections, along_a):
    groups = []
    for s in range(sections):
        for i in range(SIDE):
            ring = [(place(s, j, i) if along_a else place(s, i, j)) for j in range(SIDE)]
            groups.append([s * SIDE * SIDE + t for t in ring])
    return groups


def head_rings(sections):
    return [[(s * SIDE + g) * SIDE + i for i in range(SIDE)] for s in range(sections) for g in range(SIDE)]


def call(body, out_shape, operands, specs, flops, moved, vmem=12 << 20, **more):
    return pl.pallas_call(
        body,
        out_shape=out_shape,
        in_specs=specs,
        out_specs=jax.tree.map(lambda _: VMEM, out_shape),
        compiler_params=pltpu.CompilerParams(vmem_limit_bytes=vmem),
        cost_estimate=pl.CostEstimate(flops=flops, bytes_accessed=moved, transcendentals=0),
        **more,
    )(*operands)


def prepare_body(ids_ref, x_ref, gain_ref, query_ref, keyval_ref, pool_ref, *refs):
    packed_ref, own_ref, row_ref, packed, own, row, sems = refs
    section = lax.axis_index("section")
    odd = section % 2

    def find(k, which):
        local = ids_ref[k] - HOST_ROWS * section
        return jnp.where((local >= 0) & (local < HOST_ROWS), local, which)

    which = lax.fori_loop(0, SLOTS, find, jnp.int32(0))
    arrivals = []
    for i in range(SIDE):
        for j in range(SIDE):
            start = pl.multiple_of(jnp.where(odd == 1, SIDE * i + j, SIDE * j + i) * BLOCK, BLOCK)
            arrivals.append((query_ref.at[pl.ds(start, BLOCK)], packed.at[i, j, pl.ds(0, BLOCK)]))
            arrivals.append((keyval_ref.at[:, pl.ds(start, BLOCK)], packed.at[i, j, pl.ds(BLOCK, KV_ROWS)]))
    arrivals.append((x_ref, own.at[pl.ds(0, TOKENS)]))
    arrivals.append((pool_ref.at[which], row))
    arrivals = [pltpu.make_async_copy(src, dst, sems.at[n]) for n, (src, dst) in enumerate(arrivals)]
    for copy in arrivals:
        copy.start()
    own[TOKENS:] = jnp.broadcast_to(gain_ref[...].astype(f32), (16, BLOCK)).astype(bf16)
    leaving = []
    ready = [(packed.at[i], packed_ref.at[i], arrivals[2 * SIDE * i : 2 * SIDE * (i + 1)]) for i in range(SIDE)]
    ready += [(own, own_ref, arrivals[-2:-1]), (row, row_ref, arrivals[-1:])]
    for n, (src, dst, waits) in enumerate(ready):
        for copy in waits:
            copy.wait()
        leaving.append(pltpu.make_async_copy(src, dst, sems.at[len(arrivals) + n]))
        leaving[-1].start()
    for copy in leaving:
        copy.wait()


def prepare(row_ids, x, gain, w_query, w_kv, pool):
    packed = (SIDE, SIDE, BLOCK + KV_ROWS, BLOCK)
    own = (TOKENS + 16, BLOCK)
    row = pool.shape[1:]
    return pl.pallas_call(
        prepare_body,
        out_shape=tuple(jax.ShapeDtypeStruct(shape, bf16) for shape in (packed, own, row)),
        in_specs=[SMEM, ANY, VMEM, ANY, ANY, ANY],
        out_specs=(ANY, ANY, ANY),
        scratch_shapes=[
            pltpu.VMEM(packed, bf16),
            pltpu.VMEM(own, bf16),
            pltpu.VMEM(row, bf16),
            pltpu.SemaphoreType.DMA((2 * SIDE * SIDE + SIDE + 4,)),
        ],
        cost_estimate=pl.CostEstimate(flops=0, bytes_accessed=6 << 20, transcendentals=0),
    )(row_ids, x, gain, w_query, w_kv, pool)


def ring_place():
    section, tensor = lax.axis_index("section"), lax.axis_index("tensor")
    return jnp.where(section % 2 == 1, tensor % SIDE, tensor // SIDE)


def project_body(is_second, *refs):
    x_refs = refs[:SIDE]
    if is_second:
        gain_ref, w_ref, out_ref, wide_ref, kv_ref = refs[SIDE:]
    else:
        w_ref, out_ref, gain_ref, wide_ref, kv_ref, held, sems = refs[SIDE:]
        copies = [pltpu.make_async_copy(ref, held.at[d], sems.at[d]) for d, ref in enumerate(x_refs)]
        for copy in copies:
            copy.start()
        x_refs = [held.at[d] for d in range(SIDE)]
    here = ring_place()
    ones = jnp.ones((8, BLOCK), bf16)
    squares = jnp.zeros((8, TOKENS), f32)
    origins = [(here + SIDE - d) % SIDE for d in range(SIDE)]
    for d in range(SIDE):
        cols = slice(d * BLOCK, (d + 1) * BLOCK)
        if not is_second:
            copies[d].wait()
            gain_ref[16 * d : 16 * (d + 1)] = x_refs[d][TOKENS:]
        part = x_refs[d][:TOKENS].astype(f32)
        wide_ref[:, cols] = (part * gain_ref[16 * d : 16 * d + 1].astype(f32)).astype(bf16)
        square = part * part
        upper = square.astype(bf16)
        lower = (square - upper.astype(f32)).astype(bf16)
        squares += lax.dot_general(ones, upper, NT, preferred_element_type=f32)
        squares += lax.dot_general(ones, lower, NT, preferred_element_type=f32)
        for b in range(SIDE):
            kv_ref[b * KV_ROWS : (b + 1) * KV_ROWS, cols] = w_ref[b, origins[d], BLOCK:]
    keyval = lax.dot_general(kv_ref[...], wide_ref[...], NT, preferred_element_type=f32).astype(bf16)
    first = squares.astype(bf16)
    second = (squares - first.astype(f32)).astype(bf16)
    stats = [first[:1, :HALF], first[:1, HALF:], second[:1, :HALF], second[:1, HALF:]]
    stats = jnp.concatenate([s.astype(f32) for s in stats] + [jnp.zeros((12, HALF), f32)], axis=0).astype(bf16)
    for b in range(SIDE):
        total = jnp.zeros((TOKENS, BLOCK), f32)
        for d in range(SIDE):
            total += jnp.dot(
                wide_ref[:, d * BLOCK : (d + 1) * BLOCK],
                w_ref[b, origins[d], :BLOCK],
                preferred_element_type=f32,
            )
        out_ref[b, :TOKENS] = total.astype(bf16)
        rows = slice(b * KV_ROWS, (b + 1) * KV_ROWS)
        out_ref[b, TOKENS : TOKENS + KV_ROWS] = keyval[rows, :HALF]
        out_ref[b, TOKENS + KV_ROWS : TOKENS + 2 * KV_ROWS] = keyval[rows, HALF:]
        out_ref[b, TOKENS + 2 * KV_ROWS :] = stats


def project(is_second, blocks, gains, weights):
    parts = jax.ShapeDtypeStruct((SIDE, SENT_ROWS, BLOCK), bf16)
    return call(
        functools.partial(project_body, is_second),
        parts if is_second else (parts, jax.ShapeDtypeStruct((16 * SIDE, BLOCK), bf16)),
        (*blocks, *gains, weights),
        [VMEM if is_second else ANY] * SIDE + [VMEM] * (len(gains) + 1),
        2 * TOKENS * 1024 * 1280,
        6 << 20,
        scratch_shapes=[
            pltpu.VMEM((TOKENS, SIDE * BLOCK), bf16),
            pltpu.VMEM((SIDE * KV_ROWS, SIDE * BLOCK), bf16),
            *([] if is_second else [pltpu.VMEM((SIDE, *blocks[0].shape), bf16), pltpu.SemaphoreType.DMA((SIDE,))]),
        ],
    )


def down(row):
    return jnp.transpose(jnp.broadcast_to(row, (HEAD_DIM, HEAD_DIM)))


def combine_body(parts_ref, query_ref, keyval_ref):
    tail = parts_ref[0, TOKENS:].astype(f32)
    for b in range(1, SIDE):
        tail += parts_ref[b, TOKENS:].astype(f32)
    stats = tail[2 * KV_ROWS :]
    for h in range(2):
        mean = (stats[h : h + 1] + stats[2 + h : 3 + h]) / D
        scale = lax.rsqrt(mean + norm_eps)
        keyval = (tail[h * KV_ROWS : (h + 1) * KV_ROWS] * scale).astype(bf16)
        for b in range(SIDE):
            keyval_ref[b, :, h * HALF : (h + 1) * HALF] = keyval
        for q in range(2):
            start = h * HALF + q * HEAD_DIM
            rows = slice(start, start + HEAD_DIM)
            total = parts_ref[0, rows].astype(f32)
            for b in range(1, SIDE):
                total += parts_ref[b, rows].astype(f32)
            factor = down(scale[:, q * HEAD_DIM : (q + 1) * HEAD_DIM])
            query_ref[rows] = (total * jnp.concatenate([factor, factor], axis=1)).astype(bf16)


def combine(parts):
    return call(
        combine_body,
        (jax.ShapeDtypeStruct((TOKENS, BLOCK), bf16), jax.ShapeDtypeStruct((SIDE, KV_ROWS, TOKENS), bf16)),
        (parts,),
        [VMEM],
        TOKENS * BLOCK * 8,
        2 << 20,
    )


def combine_keyval_body(parts_ref, keyval_ref, scale_ref, held, sems):
    copies = [
        pltpu.make_async_copy(parts_ref.at[b, pl.ds(TOKENS, SENT_ROWS - TOKENS)], held.at[b], sems.at[b])
        for b in range(SIDE)
    ]
    for copy in copies:
        copy.start()
    for copy in copies:
        copy.wait()
    tail = held[0].astype(f32)
    for b in range(1, SIDE):
        tail += held[b].astype(f32)
    stats = tail[2 * KV_ROWS :]
    for h in range(2):
        cols = slice(h * HALF, (h + 1) * HALF)
        scale = lax.rsqrt((stats[h : h + 1] + stats[2 + h : 3 + h]) / D + norm_eps)
        scale_ref[:, cols] = jnp.broadcast_to(scale, (8, HALF))
        keyval = (tail[h * KV_ROWS : (h + 1) * KV_ROWS] * scale).astype(bf16)
        for b in range(SIDE):
            keyval_ref[b, :, cols] = keyval


def combine_keyval(parts):
    return call(
        combine_keyval_body,
        (jax.ShapeDtypeStruct((SIDE, KV_ROWS, TOKENS), bf16), jax.ShapeDtypeStruct((8, TOKENS), f32)),
        (parts,),
        [ANY],
        TOKENS * KV_ROWS * 8,
        1 << 19,
        vmem=61 << 20,
        scratch_shapes=[
            pltpu.VMEM((SIDE, SENT_ROWS - TOKENS, HALF), bf16),
            pltpu.SemaphoreType.DMA((SIDE,)),
        ],
    )


def combine_query_body(parts_ref, scale_ref, query_ref, held, sems):
    blocks = TOKENS // HEAD_DIM
    copies = [
        pltpu.make_async_copy(
            parts_ref.at[:, pl.ds(i * HEAD_DIM, HEAD_DIM)], held.at[:, pl.ds(i * HEAD_DIM, HEAD_DIM)], sems.at[i]
        )
        for i in range(blocks)
    ]
    for copy in copies:
        copy.start()
    for i in range(blocks):
        copies[i].wait()
        rows = slice(i * HEAD_DIM, (i + 1) * HEAD_DIM)
        total = held[0, rows].astype(f32)
        for b in range(1, SIDE):
            total += held[b, rows].astype(f32)
        factor = down(scale_ref[:1, rows])
        query_ref[rows] = (total * jnp.concatenate([factor, factor], axis=1)).astype(bf16)


def combine_query(parts, scale):
    return call(
        combine_query_body,
        jax.ShapeDtypeStruct((TOKENS, BLOCK), bf16),
        (parts, scale),
        [ANY, VMEM],
        TOKENS * BLOCK * 8,
        2 << 20,
        vmem=61 << 20,
        scratch_shapes=[pltpu.VMEM((SIDE, TOKENS, BLOCK), bf16), pltpu.SemaphoreType.DMA((TOKENS // HEAD_DIM,))],
    )


def attend_body(is_second, lengths_ref, x_ref, query_ref, keyval_ref, segments_ref, *refs):
    section = lax.axis_index("section")
    if is_second:
        (out_ref,) = refs
    else:
        *frame_refs, out_ref, sent_ref, held, sems = refs
    if is_second:
        ids = segments_ref[pl.ds(jnp.maximum(section - 1, 0), 1), :]
        spot = lax.broadcasted_iota(jnp.int32, (1, TOKENS), 1)

        def count(k, carried):
            end, slot = carried
            end = end + lengths_ref[k]
            return end, slot + (spot >= end).astype(jnp.int32)

        _, slot = lax.fori_loop(0, SLOTS, count, (jnp.int32(0), jnp.zeros((1, TOKENS), jnp.int32)))
        ids = jnp.where(section == 0, slot, ids)
    else:
        ids = segments_ref[pl.ds(section, 1), :]
    ids = ids.astype(f32)
    steps = []
    for i in range(TOKENS // HEAD_DIM):
        rows = slice(i * HEAD_DIM, (i + 1) * HEAD_DIM)
        low = max(i - 1, 0) * HEAD_DIM
        width = (i + 1) * HEAD_DIM - low
        cols = slice(low, low + width)
        own = down(ids[:, rows])
        if width > HEAD_DIM:
            own = jnp.concatenate([own, own], axis=1)
        place_r = lax.broadcasted_iota(jnp.int32, (HEAD_DIM, width), 0) + i * HEAD_DIM
        place_c = lax.broadcasted_iota(jnp.int32, (HEAD_DIM, width), 1) + low
        allowed = (own == ids[:, cols]) & (place_c <= place_r)
        keys = jnp.concatenate([keyval_ref[0, :, cols], keyval_ref[1, :, cols]], axis=0)
        for h in range(2):
            lanes = slice(h * HEAD_DIM, (h + 1) * HEAD_DIM)
            scores = jnp.dot(query_ref[rows, lanes], keys, preferred_element_type=f32) * HEAD_DIM ** (-0.5)
            steps.append((rows, cols, lanes, jnp.where(allowed, scores, masked_score)))
    for n, (rows, cols, lanes, scores) in enumerate(steps):
        grown = jnp.exp(scores - jnp.max(scores, axis=1, keepdims=True))
        weights = (grown * (1.0 / jnp.sum(grown, axis=1, keepdims=True))).astype(bf16)
        steps[n] = (rows, cols, lanes, weights)
    for rows, cols, lanes, weights in steps:
        values = jnp.concatenate([keyval_ref[2, :, cols], keyval_ref[3, :, cols]], axis=0)
        context = lax.dot_general(weights, values, NT, preferred_element_type=f32).astype(bf16)
        done = (x_ref[rows, lanes].astype(f32) + context.astype(f32)).astype(bf16)
        out_ref[rows, lanes] = done
        if not is_second:
            sent_ref[rows, lanes] = done
    if not is_second:

        @pl.when(section == lax.axis_size("section") - 1)
        def _():
            copies = [pltpu.make_async_copy(ref, held.at[n], sems.at[n]) for n, ref in enumerate(frame_refs)]
            for copy in copies:
                copy.start()
            for copy in copies:
                copy.wait()
            sent_ref[...] = functools.reduce(jnp.add, [held[n].astype(f32) for n in range(SIDE)]).astype(bf16)


def attend(is_second, lengths, x, query, keyval, segments, frames):
    made = jax.ShapeDtypeStruct((TOKENS, BLOCK), bf16)
    held = pltpu.VMEM((SIDE, TOKENS, BLOCK), bf16)
    return call(
        functools.partial(attend_body, is_second),
        made if is_second else (made, made),
        (lengths, x, query, keyval, segments, *frames),
        [SMEM] + [VMEM] * 4 + [ANY] * len(frames),
        2 * TOKENS * 256 * 128 * 4,
        1 << 20,
        scratch_shapes=[] if is_second else [held, pltpu.SemaphoreType.DMA((SIDE,))],
    )


def frame_body(ids_ref, lengths_ref, *refs):
    pair_refs, (out_ref, starts, counts, rows_ref, hits_ref) = refs[: NEAR // 2], refs[NEAR // 2 :]
    section = lax.axis_index("section")
    for n in range(NEAR):
        starts[n] = 0
        counts[n] = 0
    for n, ref in enumerate(pair_refs):
        rows_ref[2 * n * ROW_MAX : 2 * (n + 1) * ROW_MAX] = ref[...]

    def note(k, start):
        length = lengths_ref[k]
        behind = section - lax.div(ids_ref[k], HOST_ROWS)

        @pl.when((behind >= 0) & (behind < NEAR))
        def _():
            spot = behind + 1 - 2 * (behind % 2)
            starts[spot] = start
            counts[spot] = length

        return start + length

    lax.fori_loop(0, SLOTS, note, jnp.int32(0))
    offset = lax.broadcasted_iota(jnp.int32, (TOKENS, ROW_MAX), 0) - lax.broadcasted_iota(
        jnp.int32, (TOKENS, ROW_MAX), 1
    )
    col = lax.broadcasted_iota(jnp.int32, (TOKENS, ROW_MAX), 1)
    for n in range(NEAR):
        hit = (offset == starts[n]) & (col < counts[n])
        hits_ref[:, n * ROW_MAX : (n + 1) * ROW_MAX] = hit.astype(f32).astype(bf16)
    out_ref[...] = jnp.dot(hits_ref[...], rows_ref[...], preferred_element_type=f32).astype(bf16)


def make_frame(row_ids, row_lengths, rows):
    return call(
        frame_body,
        jax.ShapeDtypeStruct((TOKENS, BLOCK), bf16),
        (row_ids, row_lengths, *rows),
        [SMEM, SMEM] + [VMEM] * (NEAR // 2),
        2 * TOKENS * NEAR * 128 * 256,
        1 << 20,
        scratch_shapes=[
            pltpu.SMEM((NEAR,), jnp.int32),
            pltpu.SMEM((NEAR,), jnp.int32),
            pltpu.VMEM((NEAR * ROW_MAX, BLOCK), bf16),
            pltpu.VMEM((TOKENS, NEAR * ROW_MAX), bf16),
        ],
    )


def bring(array, sections, step, count):
    last, span = sections - 1, (count + 1) * step
    got = []
    for n in range(1, count + 1):
        route = [(i - n * step, i) for i in range(sections) if (last - i) % span == 0]
        got.append(lax.ppermute(array, "section", route))
    return got


def per_device(activations, gain, w_query, w_kv, segments, pool, row_ids, row_lengths):
    sections = lax.axis_size("section")
    ring_b, ring_y = rings(sections, False), head_rings(sections)
    barrier = lax.optimization_barrier
    grid = [(s, a, b) for s in range(sections) for a in range(SIDE) for b in range(SIDE)]

    def number(s, a, b, like):
        return s * SIDE * SIDE + place(like, a % SIDE, b)

    def exchange(array, ring):
        return lax.all_to_all(array, AXES, 0, 0, axis_index_groups=ring)

    x = activations[0]
    packed, own, row = prepare(row_ids, x, gain, w_query[0], w_kv[0], pool)
    weights = exchange(packed, ring_b)
    blocks = [own]
    for d in range(1, SIDE):
        route = [(number(s, a - d, b, s), number(s, a, b, s)) for s, a, b in grid]
        blocks.append(lax.ppermute(own, AXES, route))

    pair = jnp.concatenate([*bring(row, sections, 1, 1), row], axis=0)
    blocks[SIDE - 1], pair = barrier((blocks[SIDE - 1], pair))
    pairs = [pair, *bring(pair, sections, 2, NEAR // 2 - 1)]
    frame = make_frame(row_ids, row_lengths, pairs)
    weights, frame = barrier((weights, frame))
    frames = [frame, *bring(frame, sections, NEAR, sections // NEAR - 1)]

    parts, gains = project(False, blocks, [], weights)
    parts = exchange(parts, ring_b)
    keyval, scale = combine_keyval(parts)
    query = combine_query(parts, scale)
    first, sent = attend(False, row_lengths, x, query, exchange(keyval, ring_y), segments, frames)

    blocks = []
    for d in range(SIDE):
        route = [(number((s - 1) % sections, a - d, b, s), number(s, a, b, s)) for s, a, b in grid]
        blocks.append(lax.ppermute(sent, AXES, route))
    query, keyval = combine(exchange(project(True, blocks, [gains], weights), ring_b))
    second = attend(True, row_lengths, blocks[0], query, exchange(keyval, ring_y), segments, [])
    return first[None], second[None]


def solution(mesh):
    return jax.shard_map(
        per_device,
        mesh=mesh,
        in_specs=(
            P("section", None, "tensor"),
            P("section", "tensor"),
            P("section", None, "tensor"),
            P("section", "tensor", None),
            P(),
            P("section", None, "tensor"),
            P(),
            P(),
        ),
        out_specs=(P("section", None, "tensor"), P("section", None, "tensor")),
        check_vma=False,
    )
```

```python
import functools

import jax
import jax.numpy as jnp
from jax import lax
from jax.experimental import pallas as pl
from jax.experimental.pallas import tpu as pltpu
from jax.sharding import PartitionSpec as P

D = 4096
HEAD_DIM = 128
SIDE = 4
BLOCK = 256
KV_ROWS = 64
TOKENS = 512
HALF = 256
ROW_MAX = 128
HOST_ROWS = 2
SLOTS = 32
NEAR = 8
SENT_ROWS = TOKENS + 2 * KV_ROWS + 16
AXES = ("section", "tensor")
norm_eps = 1e-05
masked_score = -1e30
f32, bf16 = jnp.float32, jnp.bfloat16
VMEM = pl.BlockSpec(memory_space=pltpu.VMEM)
ANY = pl.BlockSpec(memory_space=pl.ANY)
SMEM = pl.BlockSpec(memory_space=pltpu.SMEM)
NT = (((1,), (1,)), ((), ()))


def place(section, first, second):
    return SIDE * first + second if section % 2 == 0 else SIDE * second + first


def rings(sections, along_a):
    groups = []
    for s in range(sections):
        for i in range(SIDE):
            ring = [(place(s, j, i) if along_a else place(s, i, j)) for j in range(SIDE)]
            groups.append([s * SIDE * SIDE + t for t in ring])
    return groups


def head_rings(sections):
    return [[(s * SIDE + g) * SIDE + i for i in range(SIDE)] for s in range(sections) for g in range(SIDE)]


def call(body, out_shape, operands, specs, flops, moved, vmem=12 << 20, **more):
    return pl.pallas_call(
        body,
        out_shape=out_shape,
        in_specs=specs,
        out_specs=jax.tree.map(lambda _: VMEM, out_shape),
        compiler_params=pltpu.CompilerParams(vmem_limit_bytes=vmem),
        cost_estimate=pl.CostEstimate(flops=flops, bytes_accessed=moved, transcendentals=0),
        **more,
    )(*operands)


def prepare_body(ids_ref, x_ref, gain_ref, query_ref, keyval_ref, pool_ref, *refs):
    packed_ref, own_ref, row_ref, packed, own, row, sems = refs
    section = lax.axis_index("section")
    odd = section % 2

    def find(k, which):
        local = ids_ref[k] - HOST_ROWS * section
        return jnp.where((local >= 0) & (local < HOST_ROWS), local, which)

    which = lax.fori_loop(0, SLOTS, find, jnp.int32(0))
    arrivals = []
    for i in range(SIDE):
        for j in range(SIDE):
            start = pl.multiple_of(jnp.where(odd == 1, SIDE * i + j, SIDE * j + i) * BLOCK, BLOCK)
            arrivals.append((query_ref.at[pl.ds(start, BLOCK)], packed.at[i, j, pl.ds(0, BLOCK)]))
            arrivals.append((keyval_ref.at[:, pl.ds(start, BLOCK)], packed.at[i, j, pl.ds(BLOCK, KV_ROWS)]))
    arrivals.append((x_ref, own.at[pl.ds(0, TOKENS)]))
    arrivals.append((pool_ref.at[which], row))
    arrivals = [pltpu.make_async_copy(src, dst, sems.at[n]) for n, (src, dst) in enumerate(arrivals)]
    for copy in arrivals:
        copy.start()
    own[TOKENS:] = jnp.broadcast_to(gain_ref[...].astype(f32), (16, BLOCK)).astype(bf16)
    leaving = []
    ready = [(packed.at[i], packed_ref.at[i], arrivals[2 * SIDE * i : 2 * SIDE * (i + 1)]) for i in range(SIDE)]
    ready += [(own, own_ref, arrivals[-2:-1]), (row, row_ref, arrivals[-1:])]
    for n, (src, dst, waits) in enumerate(ready):
        for copy in waits:
            copy.wait()
        leaving.append(pltpu.make_async_copy(src, dst, sems.at[len(arrivals) + n]))
        leaving[-1].start()
    for copy in leaving:
        copy.wait()


def prepare(row_ids, x, gain, w_query, w_kv, pool):
    packed = (SIDE, SIDE, BLOCK + KV_ROWS, BLOCK)
    own = (TOKENS + 16, BLOCK)
    row = pool.shape[1:]
    return pl.pallas_call(
        prepare_body,
        out_shape=tuple(jax.ShapeDtypeStruct(shape, bf16) for shape in (packed, own, row)),
        in_specs=[SMEM, ANY, VMEM, ANY, ANY, ANY],
        out_specs=(ANY, ANY, ANY),
        scratch_shapes=[
            pltpu.VMEM(packed, bf16),
            pltpu.VMEM(own, bf16),
            pltpu.VMEM(row, bf16),
            pltpu.SemaphoreType.DMA((2 * SIDE * SIDE + SIDE + 4,)),
        ],
        cost_estimate=pl.CostEstimate(flops=0, bytes_accessed=6 << 20, transcendentals=0),
    )(row_ids, x, gain, w_query, w_kv, pool)


def ring_place():
    section, tensor = lax.axis_index("section"), lax.axis_index("tensor")
    return jnp.where(section % 2 == 1, tensor % SIDE, tensor // SIDE)


def project_body(is_second, *refs):
    x_refs = refs[:SIDE]
    if is_second:
        gain_ref, w_ref, out_ref, kept_ref, wide_ref, kv_ref = refs[SIDE:]
        x_refs = x_refs[::-1]
        kept_ref[...] = x_refs[0][...]
    else:
        w_ref, out_ref, gain_ref, wide_ref, kv_ref, held, sems = refs[SIDE:]
        copies = [pltpu.make_async_copy(ref, held.at[d], sems.at[d]) for d, ref in enumerate(x_refs)]
        for copy in copies:
            copy.start()
        x_refs = [held.at[d] for d in range(SIDE)]
    here = ring_place()
    ones = jnp.ones((8, BLOCK), bf16)
    squares = jnp.zeros((8, TOKENS), f32)
    origins = [(here + SIDE - d) % SIDE for d in range(SIDE)]
    for d in range(SIDE):
        cols = slice(d * BLOCK, (d + 1) * BLOCK)
        if not is_second:
            copies[d].wait()
            gain_ref[16 * d : 16 * (d + 1)] = x_refs[d][TOKENS:]
        part = x_refs[d][:TOKENS].astype(f32)
        wide_ref[:, cols] = (part * gain_ref[16 * d : 16 * d + 1].astype(f32)).astype(bf16)
        square = part * part
        upper = square.astype(bf16)
        lower = (square - upper.astype(f32)).astype(bf16)
        squares += lax.dot_general(ones, upper, NT, preferred_element_type=f32)
        squares += lax.dot_general(ones, lower, NT, preferred_element_type=f32)
        for b in range(SIDE):
            kv_ref[b * KV_ROWS : (b + 1) * KV_ROWS, cols] = w_ref[b, origins[d], BLOCK:]
    keyval = lax.dot_general(kv_ref[...], wide_ref[...], NT, preferred_element_type=f32).astype(bf16)
    first = squares.astype(bf16)
    second = (squares - first.astype(f32)).astype(bf16)
    stats = [first[:1, :HALF], first[:1, HALF:], second[:1, :HALF], second[:1, HALF:]]
    stats = jnp.concatenate([s.astype(f32) for s in stats] + [jnp.zeros((12, HALF), f32)], axis=0).astype(bf16)
    for b in range(SIDE):
        total = jnp.zeros((TOKENS, BLOCK), f32)
        for d in range(SIDE):
            total += jnp.dot(
                wide_ref[:, d * BLOCK : (d + 1) * BLOCK],
                w_ref[b, origins[d], :BLOCK],
                preferred_element_type=f32,
            )
        out_ref[b, :TOKENS] = total.astype(bf16)
        rows = slice(b * KV_ROWS, (b + 1) * KV_ROWS)
        out_ref[b, TOKENS : TOKENS + KV_ROWS] = keyval[rows, :HALF]
        out_ref[b, TOKENS + KV_ROWS : TOKENS + 2 * KV_ROWS] = keyval[rows, HALF:]
        out_ref[b, TOKENS + 2 * KV_ROWS :] = stats


def project(is_second, blocks, gains, weights):
    parts = jax.ShapeDtypeStruct((SIDE, SENT_ROWS, BLOCK), bf16)
    return call(
        functools.partial(project_body, is_second),
        (parts, jax.ShapeDtypeStruct((TOKENS, BLOCK) if is_second else (16 * SIDE, BLOCK), bf16)),
        (*blocks, *gains, weights),
        [VMEM if is_second else ANY] * SIDE + [VMEM] * (len(gains) + 1),
        2 * TOKENS * 1024 * 1280,
        6 << 20,
        scratch_shapes=[
            pltpu.VMEM((TOKENS, SIDE * BLOCK), bf16),
            pltpu.VMEM((SIDE * KV_ROWS, SIDE * BLOCK), bf16),
            *([] if is_second else [pltpu.VMEM((SIDE, *blocks[0].shape), bf16), pltpu.SemaphoreType.DMA((SIDE,))]),
        ],
    )


def down(row):
    return jnp.transpose(jnp.broadcast_to(row, (HEAD_DIM, HEAD_DIM)))


def combine_body(parts_ref, query_ref, keyval_ref):
    tail = parts_ref[0, TOKENS:].astype(f32)
    for b in range(1, SIDE):
        tail += parts_ref[b, TOKENS:].astype(f32)
    stats = tail[2 * KV_ROWS :]
    for h in range(2):
        mean = (stats[h : h + 1] + stats[2 + h : 3 + h]) / D
        scale = lax.rsqrt(mean + norm_eps)
        keyval = (tail[h * KV_ROWS : (h + 1) * KV_ROWS] * scale).astype(bf16)
        for b in range(SIDE):
            keyval_ref[b, :, h * HALF : (h + 1) * HALF] = keyval
        for q in range(2):
            start = h * HALF + q * HEAD_DIM
            rows = slice(start, start + HEAD_DIM)
            total = parts_ref[0, rows].astype(f32)
            for b in range(1, SIDE):
                total += parts_ref[b, rows].astype(f32)
            factor = down(scale[:, q * HEAD_DIM : (q + 1) * HEAD_DIM])
            query_ref[rows] = (total * jnp.concatenate([factor, factor], axis=1)).astype(bf16)


def combine(parts):
    return call(
        combine_body,
        (jax.ShapeDtypeStruct((TOKENS, BLOCK), bf16), jax.ShapeDtypeStruct((SIDE, KV_ROWS, TOKENS), bf16)),
        (parts,),
        [VMEM],
        TOKENS * BLOCK * 8,
        2 << 20,
    )


def combine_keyval_body(parts_ref, keyval_ref, scale_ref, held, sems):
    copies = [
        pltpu.make_async_copy(parts_ref.at[b, pl.ds(TOKENS, SENT_ROWS - TOKENS)], held.at[b], sems.at[b])
        for b in range(SIDE)
    ]
    for copy in copies:
        copy.start()
    for copy in copies:
        copy.wait()
    tail = held[0].astype(f32)
    for b in range(1, SIDE):
        tail += held[b].astype(f32)
    stats = tail[2 * KV_ROWS :]
    for h in range(2):
        cols = slice(h * HALF, (h + 1) * HALF)
        scale = lax.rsqrt((stats[h : h + 1] + stats[2 + h : 3 + h]) / D + norm_eps)
        scale_ref[:, cols] = jnp.broadcast_to(scale, (8, HALF))
        keyval = (tail[h * KV_ROWS : (h + 1) * KV_ROWS] * scale).astype(bf16)
        for b in range(SIDE):
            keyval_ref[b, :, cols] = keyval


def combine_keyval(parts):
    return call(
        combine_keyval_body,
        (jax.ShapeDtypeStruct((SIDE, KV_ROWS, TOKENS), bf16), jax.ShapeDtypeStruct((8, TOKENS), f32)),
        (parts,),
        [ANY],
        TOKENS * KV_ROWS * 8,
        1 << 19,
        vmem=60 << 20,
        scratch_shapes=[
            pltpu.VMEM((SIDE, SENT_ROWS - TOKENS, HALF), bf16),
            pltpu.SemaphoreType.DMA((SIDE,)),
        ],
    )


def combine_query_body(parts_ref, scale_ref, query_ref, held, sems):
    blocks = TOKENS // HEAD_DIM
    copies = [
        pltpu.make_async_copy(
            parts_ref.at[:, pl.ds(i * HEAD_DIM, HEAD_DIM)], held.at[:, pl.ds(i * HEAD_DIM, HEAD_DIM)], sems.at[i]
        )
        for i in range(blocks)
    ]
    for copy in copies:
        copy.start()
    for i in range(blocks):
        copies[i].wait()
        rows = slice(i * HEAD_DIM, (i + 1) * HEAD_DIM)
        total = held[0, rows].astype(f32)
        for b in range(1, SIDE):
            total += held[b, rows].astype(f32)
        factor = down(scale_ref[:1, rows])
        query_ref[rows] = (total * jnp.concatenate([factor, factor], axis=1)).astype(bf16)


def combine_query(parts, scale):
    return call(
        combine_query_body,
        jax.ShapeDtypeStruct((TOKENS, BLOCK), bf16),
        (parts, scale),
        [ANY, VMEM],
        TOKENS * BLOCK * 8,
        2 << 20,
        vmem=60 << 20,
        scratch_shapes=[pltpu.VMEM((SIDE, TOKENS, BLOCK), bf16), pltpu.SemaphoreType.DMA((TOKENS // HEAD_DIM,))],
    )


def attend_body(is_second, lengths_ref, x_ref, query_ref, keyval_ref, segments_ref, *refs):
    section = lax.axis_index("section")
    if is_second:
        (out_ref,) = refs
    else:
        *frame_refs, out_ref, sent_ref, held, sems = refs
    if is_second:
        ids = segments_ref[pl.ds(jnp.maximum(section - 1, 0), 1), :]
        spot = lax.broadcasted_iota(jnp.int32, (1, TOKENS), 1)

        def count(k, carried):
            end, slot = carried
            end = end + lengths_ref[k]
            return end, slot + (spot >= end).astype(jnp.int32)

        _, slot = lax.fori_loop(0, SLOTS, count, (jnp.int32(0), jnp.zeros((1, TOKENS), jnp.int32)))
        ids = jnp.where(section == 0, slot, ids)
    else:
        ids = segments_ref[pl.ds(section, 1), :]
    ids = ids.astype(f32)
    steps = []
    for i in range(TOKENS // HEAD_DIM):
        rows = slice(i * HEAD_DIM, (i + 1) * HEAD_DIM)
        low = max(i - 1, 0) * HEAD_DIM
        width = (i + 1) * HEAD_DIM - low
        cols = slice(low, low + width)
        own = down(ids[:, rows])
        if width > HEAD_DIM:
            own = jnp.concatenate([own, own], axis=1)
        place_r = lax.broadcasted_iota(jnp.int32, (HEAD_DIM, width), 0) + i * HEAD_DIM
        place_c = lax.broadcasted_iota(jnp.int32, (HEAD_DIM, width), 1) + low
        allowed = (own == ids[:, cols]) & (place_c <= place_r)
        keys = jnp.concatenate([keyval_ref[0, :, cols], keyval_ref[1, :, cols]], axis=0)
        for h in range(2):
            lanes = slice(h * HEAD_DIM, (h + 1) * HEAD_DIM)
            scores = jnp.dot(query_ref[rows, lanes], keys, preferred_element_type=f32) * HEAD_DIM ** (-0.5)
            steps.append((rows, cols, lanes, jnp.where(allowed, scores, masked_score)))
    for n, (rows, cols, lanes, scores) in enumerate(steps):
        grown = jnp.exp(scores - jnp.max(scores, axis=1, keepdims=True))
        weights = (grown * (1.0 / jnp.sum(grown, axis=1, keepdims=True))).astype(bf16)
        steps[n] = (rows, cols, lanes, weights)
    for rows, cols, lanes, weights in steps:
        values = jnp.concatenate([keyval_ref[2, :, cols], keyval_ref[3, :, cols]], axis=0)
        context = lax.dot_general(weights, values, NT, preferred_element_type=f32).astype(bf16)
        done = (x_ref[rows, lanes].astype(f32) + context.astype(f32)).astype(bf16)
        out_ref[rows, lanes] = done
        if not is_second:
            sent_ref[rows, lanes] = done
    if not is_second:

        @pl.when(section == lax.axis_size("section") - 1)
        def _():
            copies = [pltpu.make_async_copy(ref, held.at[n], sems.at[n]) for n, ref in enumerate(frame_refs)]
            for copy in copies:
                copy.start()
            for copy in copies:
                copy.wait()
            sent_ref[...] = functools.reduce(jnp.add, [held[n].astype(f32) for n in range(SIDE)]).astype(bf16)


def attend(is_second, lengths, x, query, keyval, segments, frames):
    made = jax.ShapeDtypeStruct((TOKENS, BLOCK), bf16)
    held = pltpu.VMEM((SIDE, TOKENS, BLOCK), bf16)
    return call(
        functools.partial(attend_body, is_second),
        made if is_second else (made, made),
        (lengths, x, query, keyval, segments, *frames),
        [SMEM] + [VMEM] * 4 + [ANY] * len(frames),
        2 * TOKENS * 256 * 128 * 4,
        1 << 20,
        scratch_shapes=[] if is_second else [held, pltpu.SemaphoreType.DMA((SIDE,))],
    )


def frame_body(ids_ref, lengths_ref, *refs):
    pair_refs, (out_ref, starts, counts, rows_ref, hits_ref) = refs[: NEAR // 2], refs[NEAR // 2 :]
    section = lax.axis_index("section")
    for n in range(NEAR):
        starts[n] = 0
        counts[n] = 0
    for n, ref in enumerate(pair_refs):
        rows_ref[2 * n * ROW_MAX : 2 * (n + 1) * ROW_MAX] = ref[...]

    def note(k, start):
        length = lengths_ref[k]
        behind = section - lax.div(ids_ref[k], HOST_ROWS)

        @pl.when((behind >= 0) & (behind < NEAR))
        def _():
            spot = behind + 1 - 2 * (behind % 2)
            starts[spot] = start
            counts[spot] = length

        return start + length

    lax.fori_loop(0, SLOTS, note, jnp.int32(0))
    offset = lax.broadcasted_iota(jnp.int32, (TOKENS, ROW_MAX), 0) - lax.broadcasted_iota(
        jnp.int32, (TOKENS, ROW_MAX), 1
    )
    col = lax.broadcasted_iota(jnp.int32, (TOKENS, ROW_MAX), 1)
    for n in range(NEAR):
        hit = (offset == starts[n]) & (col < counts[n])
        hits_ref[:, n * ROW_MAX : (n + 1) * ROW_MAX] = hit.astype(f32).astype(bf16)
    out_ref[...] = jnp.dot(hits_ref[...], rows_ref[...], preferred_element_type=f32).astype(bf16)


def make_frame(row_ids, row_lengths, rows):
    return call(
        frame_body,
        jax.ShapeDtypeStruct((TOKENS, BLOCK), bf16),
        (row_ids, row_lengths, *rows),
        [SMEM, SMEM] + [VMEM] * (NEAR // 2),
        2 * TOKENS * NEAR * 128 * 256,
        1 << 20,
        scratch_shapes=[
            pltpu.SMEM((NEAR,), jnp.int32),
            pltpu.SMEM((NEAR,), jnp.int32),
            pltpu.VMEM((NEAR * ROW_MAX, BLOCK), bf16),
            pltpu.VMEM((TOKENS, NEAR * ROW_MAX), bf16),
        ],
    )


def bring(array, sections, step, count):
    last, span = sections - 1, (count + 1) * step
    got = []
    for n in range(1, count + 1):
        route = [(i - n * step, i) for i in range(sections) if (last - i) % span == 0]
        got.append(lax.ppermute(array, "section", route))
    return got


def per_device(activations, gain, w_query, w_kv, segments, pool, row_ids, row_lengths):
    sections = lax.axis_size("section")
    ring_b, ring_y = rings(sections, False), head_rings(sections)
    barrier = lax.optimization_barrier
    grid = [(s, a, b) for s in range(sections) for a in range(SIDE) for b in range(SIDE)]

    def number(s, a, b, like):
        return s * SIDE * SIDE + place(like, a % SIDE, b)

    def exchange(array, ring):
        return lax.all_to_all(array, AXES, 0, 0, axis_index_groups=ring)

    x = activations[0]
    packed, own, row = prepare(row_ids, x, gain, w_query[0], w_kv[0], pool)
    weights = exchange(packed, ring_b)
    blocks = [own]
    for d in range(1, SIDE):
        route = [(number(s, a - d, b, s), number(s, a, b, s)) for s, a, b in grid]
        blocks.append(lax.ppermute(own, AXES, route))

    pair = jnp.concatenate([*bring(row, sections, 1, 1), row], axis=0)
    blocks[SIDE - 1], pair = barrier((blocks[SIDE - 1], pair))
    pairs = [pair, *bring(pair, sections, 2, NEAR // 2 - 1)]
    frame = make_frame(row_ids, row_lengths, pairs)
    weights, frame = barrier((weights, frame))
    frames = [frame, *bring(frame, sections, NEAR, sections // NEAR - 1)]

    parts, gains = project(False, blocks, [], weights)
    parts = exchange(parts, ring_b)
    keyval, scale = combine_keyval(parts)
    query = combine_query(parts, scale)
    first, sent = attend(False, row_lengths, x, query, exchange(keyval, ring_y), segments, frames)

    blocks = []
    for d in range(SIDE):
        route = [(number((s - 1) % sections, a - d, b, s), number(s, a, b, s)) for s, a, b in grid]
        blocks.append(lax.ppermute(sent, AXES, route))
    parts, kept = project(True, blocks[::-1], [gains], weights)
    query, keyval = combine(exchange(parts, ring_b))
    second = attend(True, row_lengths, kept, query, exchange(keyval, ring_y), segments, [])
    return first[None], second[None]


def solution(mesh):
    return jax.shard_map(
        per_device,
        mesh=mesh,
        in_specs=(
            P("section", None, "tensor"),
            P("section", "tensor"),
            P("section", None, "tensor"),
            P("section", "tensor", None),
            P(),
            P("section", None, "tensor"),
            P(),
            P(),
        ),
        out_specs=(P("section", None, "tensor"), P("section", None, "tensor")),
        check_vma=False,
    )
```
